128 devices in a mesh: segment: 8 (over x, core), strip: 16 (over z, y).
Axes of the slice: x: 4, y: 4, z: 4, core: 2. Of those that a mesh axis runs over, the one named last changes fastest.
Arguments:
- held_blocks: bfloat16 [8, 4, 128, 12, 384], P('segment', None, 'strip'), may hold values from -6 to 6
- incoming: bfloat16 [1, 4, 128, 12, 384], P(None, None, 'strip'), may hold values from -6 to 6
- frame_counts: int32 [9], replicated, may hold values from 1 to 4, as said below
- first_cache: bfloat16 [8, 2, 128, 12, 384], P('segment', None, 'strip'), may hold values from -0.25 to 2
- second_cache: bfloat16 [8, 2, 128, 12, 384], P('segment', None, 'strip'), may hold values from -0.25 to 2
- first_kernel: bfloat16 [8, 3, 3, 3, 384, 384], P('segment'), may hold values from -0.0625 to 0.0625
- first_bias: float32 [8, 384], P('segment'), may hold values from -3 to 3
- first_gain: float32 [8, 384], P('segment'), may hold values from 0.5 to 2
- second_kernel: bfloat16 [8, 3, 3, 3, 384, 384], P('segment'), may hold values from -0.0625 to 0.0625
- second_bias: float32 [8, 384], P('segment'), may hold values from -3 to 3
- second_gain: float32 [8, 384], P('segment'), may hold values from 0.5 to 2
Outputs:
- section_out: bfloat16 [2, 8, 4, 128, 12, 384], P(None, 'segment', None, 'strip')
- first_cache_out: bfloat16 [8, 2, 128, 12, 384], P('segment', None, 'strip')
- second_cache_out: bfloat16 [8, 2, 128, 12, 384], P('segment', None, 'strip')
The draws below stay inside these ranges and needn't reach their ends.
Inputs may be any that keep to these rules, and one draw needn't show every extreme that they name: `frame_counts`: the section at segment index s works at tick t (from 0) on block 7 - s + t; both 1 and 4 occur in every draw.
All inputs are finite; a program needn't handle non-finite values.
Results may differ from the reference program's by a relative error of at most 0.0051.
Values may be sent and summed in bfloat16 or wider, within the bound.
No kernel may reach another device: no remote copies, remote signals or barrier semaphores. Data moves between devices by JAX's collectives and lax.ppermute only.
A program may use at most 128 MiB of HBM per device.

```python
import math
import jax
import jax.numpy as jnp
from jax import lax

C = 384
FMAX = 4
TICKS = 2
COLS = 12
HEIGHT = 128
SECTIONS = 8
BLOCKS = 9


def draw_frame_counts(key, part):
    counts = jax.random.randint(jax.random.fold_in(key, 11), (BLOCKS,), 1, FMAX + 1)
    top_place = jax.random.randint(jax.random.fold_in(key, 12), (), 0, BLOCKS)
    low_offset = jax.random.randint(jax.random.fold_in(key, 13), (), 1, BLOCKS)
    low_place = (top_place + low_offset) % BLOCKS
    positions = jnp.arange(BLOCKS)
    counts = jnp.where(positions == top_place, FMAX, counts)
    counts = jnp.where(positions == low_place, 1, counts)
    return counts.astype(jnp.int32)


def shard_levels(rng, shape, pieces, least, top_value):
    loudness, own = 1.0, jax.random.fold_in(rng, 6)
    for axis_at, blocks in pieces:
        steps = jnp.exp(jax.random.uniform(jax.random.fold_in(own, axis_at), (blocks,), jnp.float32, least / len(pieces), top_value / len(pieces)))
        loudness = loudness * jnp.repeat(steps, shape[axis_at] // blocks).reshape([-1 if axis == axis_at else 1 for axis in range(len(shape))])
    return loudness


def gaussian(key, dims, deviation, most, cuts=(), held_as=jnp.bfloat16):
    array = deviation * jax.random.normal(key, dims, jnp.float32)
    if cuts:
        array = array * shard_levels(key, dims, cuts, -0.22, 0.18)
    return jnp.clip(array, -most, most).astype(held_as)


def setup_inputs(seed: int = 0) -> dict:
    splits = jax.random.split(jax.random.key(seed), 12)
    return {
        "held_blocks": gaussian(splits[0], (SECTIONS, FMAX, HEIGHT, COLS, C), 1.0, 6.0, ((0, 8), (2, 16))),
        "incoming": gaussian(splits[1], (TICKS - 1, FMAX, HEIGHT, COLS, C), 1.0, 6.0, ((2, 16),)),
        "frame_counts": draw_frame_counts(jax.random.fold_in(splits[11], 71), 0),
        "first_cache": jnp.clip(-0.25 + 2.25 * jax.random.uniform(splits[3], (SECTIONS, 2, HEIGHT, COLS, C), jnp.float32) ** shard_levels(splits[3], (SECTIONS, 2, HEIGHT, COLS, C), ((0, 8), (2, 16)), -0.2, 0.2), -0.25, 2.0).astype(jnp.bfloat16),
        "second_cache": jnp.clip(-0.25 + 2.25 * jax.random.uniform(splits[4], (SECTIONS, 2, HEIGHT, COLS, C), jnp.float32) ** shard_levels(splits[4], (SECTIONS, 2, HEIGHT, COLS, C), ((0, 8), (2, 16)), -0.2, 0.2), -0.25, 2.0).astype(jnp.bfloat16),
        "first_kernel": gaussian(splits[5], (SECTIONS, 3, 3, 3, C, C), (27 * C) ** -0.5, 0.0625, ((0, 8),)),
        "first_bias": gaussian(splits[6], (SECTIONS, C), 0.5, 3.0, ((0, 8),), jnp.float32),
        "first_gain": jnp.clip(jnp.exp(math.log(2.0) - 1.3862944 * jax.random.uniform(splits[7], (SECTIONS, C), jnp.float32) ** shard_levels(splits[7], (SECTIONS, C), ((0, 8),), -0.2, 0.2)), 0.5, 2.0),
        "second_kernel": gaussian(splits[8], (SECTIONS, 3, 3, 3, C, C), (27 * C) ** -0.5, 0.0625, ((0, 8),)),
        "second_bias": gaussian(splits[9], (SECTIONS, C), 0.5, 3.0, ((0, 8),), jnp.float32),
        "second_gain": jnp.clip(jnp.exp(math.log(2.0) - 1.3862944 * jax.random.uniform(splits[10], (SECTIONS, C), jnp.float32) ** shard_levels(splits[10], (SECTIONS, C), ((0, 8),), -0.2, 0.2)), 0.5, 2.0),
    }


EPSILON = 1e-06

def normed(values, channel_gain):
    factor = lax.rsqrt(lax.optimization_barrier(jnp.mean(values * values, axis=-1, keepdims=True)) + EPSILON)
    return jax.nn.silu(values * factor * channel_gain)

def convolve(window, kernel, frames):
    out_rows = window.shape[1] - 2
    breadth = window.shape[2]
    channels = kernel.shape[-1]
    padded = jnp.pad(window, ((0, 0), (0, 0), (1, 1), (0, 0)))
    summed = jnp.zeros((frames * out_rows * breadth, channels), jnp.float32)
    for time_tap in range(3):
        for row_tap in range(3):
            stacked = jnp.concatenate([padded[time_tap:time_tap + frames, row_tap:row_tap + out_rows, col_tap:col_tap + breadth] for col_tap in range(3)], axis=-1)
            summed = summed + jnp.dot(stacked.reshape(-1, 3 * channels), kernel[time_tap, row_tap].reshape(3 * channels, channels), preferred_element_type=jnp.float32)
    return summed.reshape(frames, out_rows, breadth, channels)

def section(current, live_count, first_cache, second_cache, first_kernel, first_bias, first_gain, second_kernel, second_bias, second_gain):
    frames = current.shape[0]
    live_mask = (jnp.arange(frames) < live_count)[:, None, None, None]
    inputs = jnp.where(live_mask, current.astype(jnp.float32), 0.0)
    first_in = normed(inputs, first_gain).astype(jnp.bfloat16)
    first_window = jnp.concatenate([first_cache, first_in], axis=0)
    first_rimmed = jnp.pad(first_window, ((0, 0), (1, 1), (0, 0), (0, 0)))
    hidden = jnp.where(live_mask, convolve(first_rimmed, first_kernel, frames) + first_bias, 0.0)
    second_in = normed(hidden, second_gain).astype(jnp.bfloat16)
    second_window = jnp.concatenate([second_cache, second_in], axis=0)
    second_rimmed = jnp.pad(second_window, ((0, 0), (1, 1), (0, 0), (0, 0)))
    result = jnp.where(live_mask, inputs + convolve(second_rimmed, second_kernel, frames) + second_bias, 0.0).astype(jnp.bfloat16)
    first_next = lax.dynamic_slice_in_dim(first_window, live_count, 2, 0)
    second_next = lax.dynamic_slice_in_dim(second_window, live_count, 2, 0)
    return (result, first_next, second_next)

def reference(held_blocks, incoming, frame_counts, first_cache, second_cache, first_kernel, first_bias, first_gain, second_kernel, second_bias, second_gain):
    sections = held_blocks.shape[0]
    current = held_blocks
    first_state = first_cache
    second_state = second_cache
    produced = []
    for tick_index in range(TICKS):
        if tick_index > 0:
            current = jnp.concatenate([incoming[tick_index - 1][None], produced[-1][:-1]], axis=0)
        counts_now = frame_counts[tick_index:tick_index + sections][::-1].astype(jnp.int32)

        def advance(carried, members):
            outcome = section(members[0], members[1], members[2], members[3], members[4], members[5], members[6], members[7], members[8], members[9])
            return (carried, outcome)
        unused, stacked_out = lax.scan(advance, jnp.zeros((), jnp.int32), (current, counts_now, first_state, second_state, first_kernel, first_bias, first_gain, second_kernel, second_bias, second_gain))
        outputs, first_state, second_state = stacked_out
        produced.append(outputs)
    return (jnp.stack(produced), first_state, second_state)
```

```python
import jax
import jax.numpy as jnp
from jax import lax
from jax.experimental import pallas as pl
from jax.experimental.pallas import tpu as pltpu
from jax.sharding import PartitionSpec as P

EPSILON = 1e-06
C = 384
FRAMES = 4
COLS = 12
ROWS = 8
MAIN = COLS * ROWS
EDGE = COLS * 2
BLOCK = 128
TAPS = 9
K = TAPS * C
BF16 = jnp.bfloat16
F32 = jnp.float32
VMEM = pl.BlockSpec(memory_space=pltpu.VMEM)
SMEM = pl.BlockSpec(memory_space=pltpu.SMEM)
ANY = pl.BlockSpec(memory_space=pl.ANY)


def rolled(value, shift, axis):
    shift = shift % value.shape[axis]
    return pltpu.roll(value, shift, axis) if shift else value


def rows_out(main, first):
    split = main.reshape(3, 4, ROWS, C)
    group = lax.broadcasted_iota(jnp.int32, (3, ROWS, C), 1) // 2
    out = None
    for q in range(4):
        piece = rolled(split[:, q], 2 * q - first, 1)
        out = piece if out is None else jnp.where(group == q, piece, out)
    return out.reshape(EDGE, C)


def spread(edge, which, to):
    split = edge.reshape(3, ROWS, C)
    pieces = [rolled(split, to - (2 * q + which), 1) for q in range(4)]
    return jnp.stack(pieces, axis=1).reshape(COLS, ROWS, C)


def shifted_rows(main, before, before_which, after, after_which):
    split = main.reshape(COLS, ROWS, C)
    place = lax.broadcasted_iota(jnp.int32, (COLS, ROWS, C), 1)
    down = jnp.where(place == 0, spread(before, before_which, 0), rolled(split, 1, 1))
    up = jnp.where(place == ROWS - 1, spread(after, after_which, ROWS - 1), rolled(split, -1, 1))
    return [down.reshape(MAIN, C), main, up.reshape(MAIN, C)]


def column_taps(main):
    zeros = jnp.zeros((ROWS, C), F32)
    return [
        jnp.concatenate([zeros, main[: MAIN - ROWS]], axis=0),
        main,
        jnp.concatenate([main[ROWS:], zeros], axis=0),
    ]


def edge_column_taps(edge):
    place = lax.broadcasted_iota(jnp.int32, (EDGE, C), 0)
    return [
        jnp.where(place < 2, 0.0, rolled(edge, 2, 0)),
        edge,
        jnp.where(place >= EDGE - 2, 0.0, rolled(edge, -2, 0)),
    ]


def edge_pair(top, bottom):
    even = lax.broadcasted_iota(jnp.int32, (EDGE, C), 0) % 2 == 0
    return jnp.where(even, rolled(top, -1, 0), rolled(bottom, 1, 0))


def normed(values, gain):
    factor = lax.rsqrt(jnp.mean(values * values, axis=-1, keepdims=True) + EPSILON)
    v = values * factor * gain
    return v / (1.0 + jnp.exp(-v))


def build_first(window, operand, frame):
    main = window[frame, 0:MAIN].astype(F32)
    halo = window[frame, MAIN : MAIN + 2 * EDGE].astype(F32)
    top, bottom = halo[:EDGE], halo[EDGE:]
    even = lax.broadcasted_iota(jnp.int32, (EDGE, C), 0) % 2 == 0
    mains = shifted_rows(main, top, 1, bottom, 0)
    edges = [
        jnp.where(even, top, rows_out(main, 6)),
        edge_pair(top, bottom),
        jnp.where(even, rows_out(main, 0), bottom),
    ]
    zeros = jnp.zeros((BLOCK - MAIN - EDGE, C), F32)
    for b in range(3):
        for c, (m, e) in enumerate(zip(column_taps(mains[b]), edge_column_taps(edges[b]))):
            at = (3 * b + c) * C
            operand[frame, :, at : at + C] = jnp.concatenate([m, e, zeros], axis=0).astype(BF16)


def build_second(window, operand, frame):
    main = window[frame, 0:MAIN].astype(F32)
    edge = window[frame, MAIN:BLOCK].astype(F32)[:EDGE]
    mains = shifted_rows(main, edge, 0, edge, 1)
    for b in range(3):
        for c, m in enumerate(column_taps(mains[b])):
            at = (3 * b + c) * C
            operand[frame, :, at : at + C] = m.astype(BF16)


def pack_kernel(x, first, second, up, down):
    for source, start in ((x, 0), (first, 4), (second, 6)):
        for f in range(source.shape[0]):
            main = source[f].astype(F32)
            up[start + f] = rows_out(main, 0).astype(BF16)
            down[start + f] = rows_out(main, 6).astype(BF16)


def tick_kernel(tick, *refs):
    if tick == 0:
        (counts, x, tops, bottoms, first_cache, second_cache, incoming, first_w, first_bias, first_gain, second_w,
         second_bias, second_gain, out, send, send_up, send_down, first_next, first_halo, second_next, second_edge,
         *scratch) = refs
    else:
        (counts, x, tops, bottoms, first_cache, first_cache_halo, second_cache, second_cache_edge, first_w, first_bias,
         first_gain, second_w, second_bias, second_gain, out, first_next, second_next, *scratch) = refs
    window1, window2, operand1, operand2, sums1, sums2, weights1, weights2, sems = scratch
    copies = []
    for i in range(3):
        copies.append(pltpu.make_async_copy(first_w.at[i], weights1.at[i], sems.at[i]))
    for i in range(3):
        copies.append(pltpu.make_async_copy(second_w.at[i], weights2.at[i], sems.at[3 + i]))
    for copy in copies:
        copy.start()
    segment = lax.axis_index("segment")
    strip = lax.axis_index("strip")
    live = counts[7 - segment + tick]

    window1[0:2, 0:MAIN] = first_cache[...]
    if tick == 0:
        window1[0:2, MAIN : MAIN + EDGE] = tops[4:6]
        window1[0:2, MAIN + EDGE : MAIN + 2 * EDGE] = bottoms[4:6]
    else:
        window1[0:2, MAIN : MAIN + 2 * EDGE] = first_cache_halo[...]
    gain1 = first_gain[...]

    @pl.loop(0, FRAMES)
    def _(f):
        keep = f < live
        for source, at, length in ((x, 0, MAIN), (tops, MAIN, EDGE), (bottoms, MAIN + EDGE, EDGE)):
            values = jnp.where(keep, source[f].astype(F32), 0.0)
            window1[f + 2, at : at + length] = normed(values, gain1).astype(BF16)

    @pl.loop(0, FRAMES + 2)
    def _(g):
        build_first(window1, operand1, g)

    for a in range(3):
        copies[a].wait()
        lhs = operand1[a : a + FRAMES].reshape(FRAMES * BLOCK, K)
        product = jnp.dot(lhs, weights1[a], preferred_element_type=F32)
        if a == 0:
            sums1[...] = product
        else:
            sums1[...] += product

    window2[0:2, 0:MAIN] = second_cache[...]
    if tick == 0:
        for f in range(2):
            edge = edge_pair(tops[6 + f].astype(F32), bottoms[6 + f].astype(F32))
            window2[f, MAIN : MAIN + EDGE] = edge.astype(BF16)
    else:
        window2[0:2, MAIN : MAIN + EDGE] = second_cache_edge[...]
    gain2 = second_gain[...]
    bias1 = first_bias[...]
    place = lax.broadcasted_iota(jnp.int32, (BLOCK, C), 0)
    outside = (place >= MAIN) & (
        ((place % 2 == 0) & (strip == 0)) | ((place % 2 == 1) & (strip == lax.axis_size("strip") - 1))
    )

    @pl.loop(0, FRAMES)
    def _(f):
        at = pl.multiple_of(f * BLOCK, BLOCK)
        hidden = sums1[pl.ds(at, BLOCK)] + bias1
        hidden = jnp.where(outside | (f >= live), 0.0, hidden)
        window2[f + 2] = normed(hidden, gain2).astype(BF16)

    @pl.loop(0, FRAMES + 2)
    def _(g):
        build_second(window2, operand2, g)

    for a in range(3):
        copies[3 + a].wait()
        lhs = operand2[a : a + FRAMES].reshape(FRAMES * MAIN, K)
        product = jnp.dot(lhs, weights2[a], preferred_element_type=F32)
        if a == 0:
            sums2[...] = product
        else:
            sums2[...] += product
    bias2 = second_bias[...]

    @pl.loop(0, FRAMES)
    def _(f):
        at = pl.multiple_of(f * MAIN, MAIN)
        keep = f < live
        result = sums2[pl.ds(at, MAIN)] + bias2 + x[f].astype(F32)
        result = jnp.where(keep, result, 0.0).astype(BF16)
        out[f] = result
        if tick == 0:
            passed = jnp.where(segment == lax.axis_size("segment") - 1, incoming[f].astype(F32), result.astype(F32))
            send[f] = passed.astype(BF16)
            send_up[f] = rows_out(passed, 0).astype(BF16)
            send_down[f] = rows_out(passed, 6).astype(BF16)

    for i in range(2):
        first_next[i] = window1[live + i, 0:MAIN]
        second_next[i] = window2[live + i, 0:MAIN]
        if tick == 0:
            first_halo[i] = window1[live + i, MAIN : MAIN + 2 * EDGE]
            second_edge[i] = window2[live + i, MAIN : MAIN + EDGE]


def shape(*dims):
    return jax.ShapeDtypeStruct(dims, BF16)


def run_tick(tick, operands, out_shapes):
    places = [VMEM] * len(operands)
    places[0] = SMEM
    for i in (-6, -3):
        places[i] = ANY
    return pl.pallas_call(
        lambda *refs: tick_kernel(tick, *refs),
        out_shape=out_shapes,
        in_specs=places,
        out_specs=[VMEM] * len(out_shapes),
        scratch_shapes=[
            pltpu.VMEM((FRAMES + 2, MAIN + 2 * EDGE, C), BF16),
            pltpu.VMEM((FRAMES + 2, BLOCK, C), BF16),
            pltpu.VMEM((FRAMES + 2, BLOCK, K), BF16),
            pltpu.VMEM((FRAMES + 2, MAIN, K), BF16),
            pltpu.VMEM((FRAMES * BLOCK, C), F32),
            pltpu.VMEM((FRAMES * MAIN, C), F32),
            pltpu.VMEM((3, K, C), BF16),
            pltpu.VMEM((3, K, C), BF16),
            pltpu.SemaphoreType.DMA((6,)),
        ],
        compiler_params=pltpu.CompilerParams(vmem_limit_bytes=56 << 20),
        name=f"tick{tick}",
    )(*operands)


def flat(array):
    frames = array.shape[0]
    return array.transpose(0, 2, 1, 3).reshape(frames, MAIN, C)


def unflat(array):
    frames = array.shape[0]
    return array.reshape(frames, COLS, ROWS, C).transpose(0, 2, 1, 3)


def on_device(
    held_blocks,
    incoming,
    frame_counts,
    first_cache,
    second_cache,
    first_kernel,
    first_bias,
    first_gain,
    second_kernel,
    second_bias,
    second_gain,
):
    segments = lax.axis_size("segment")
    strips = lax.axis_size("strip")
    x = flat(held_blocks[0])
    fresh = flat(incoming[0])
    first = flat(first_cache[0])
    second = flat(second_cache[0])
    params = (
        first_kernel[0].reshape(3, K, C),
        first_bias,
        first_gain,
        second_kernel[0].reshape(3, K, C),
        second_bias,
        second_gain,
    )
    up, down = pl.pallas_call(
        pack_kernel, out_shape=[shape(8, EDGE, C)] * 2, in_specs=[VMEM] * 3, out_specs=[VMEM] * 2, name="pack"
    )(x, first, second)
    forward = [(i, i + 1) for i in range(strips - 1)]
    backward = [(j, i) for i, j in forward]
    tops = lax.ppermute(down, "strip", forward)
    bottoms = lax.ppermute(up, "strip", backward)
    out0, send, send_up, send_down, first, first_halo, second, second_edge = run_tick(
        0,
        (frame_counts, x, tops, bottoms, first, second, fresh, *params),
        [shape(FRAMES, MAIN, C)] * 2
        + [shape(FRAMES, EDGE, C)] * 2
        + [shape(2, MAIN, C), shape(2, 2 * EDGE, C), shape(2, MAIN, C), shape(2, EDGE, C)],
    )

    def pairs(step):
        return [
            (s * strips + k, (s + 1) % segments * strips + k + step)
            for s in range(segments)
            for k in range(strips)
            if 0 <= k + step < strips
        ]

    axes = ("segment", "strip")
    tops = lax.ppermute(send_down, axes, pairs(1))
    bottoms = lax.ppermute(send_up, axes, pairs(-1))
    x = lax.ppermute(send, axes, pairs(0))
    out1, first, second = run_tick(
        1,
        (frame_counts, x, tops, bottoms, first, first_halo, second, second_edge, *params),
        [shape(FRAMES, MAIN, C), shape(2, MAIN, C), shape(2, MAIN, C)],
    )
    return (
        jnp.stack([unflat(out0), unflat(out1)])[:, None],
        unflat(first)[None],
        unflat(second)[None],
    )


def solution(mesh):
    return jax.shard_map(
        on_device,
        mesh=mesh,
        in_specs=(
            P("segment", None, "strip", None, None),
            P(None, None, "strip", None, None),
            P(),
            P("segment", None, "strip", None, None),
            P("segment", None, "strip", None, None),
            P("segment", None, None, None, None, None),
            P("segment", None),
            P("segment", None),
            P("segment", None, None, None, None, None),
            P("segment", None),
            P("segment", None),
        ),
        out_specs=(
            P(None, "segment", None, "strip", None, None),
            P("segment", None, "strip", None, None),
            P("segment", None, "strip", None, None),
        ),
        check_vma=False,
    )
```

```python
import jax
import jax.numpy as jnp
from jax import lax
from jax.experimental import pallas as pl
from jax.experimental.pallas import tpu as pltpu
from jax.sharding import PartitionSpec as P

EPSILON = 1e-06
C = 384
FRAMES = 4
COLS = 12
ROWS = 8
MAIN = COLS * ROWS
EDGE = COLS * 2
TAPS = 9
K = TAPS * C
TILE = 256
STEPS = -(-K // TILE)
BF16 = jnp.bfloat16
F32 = jnp.float32
VMEM = pl.BlockSpec(memory_space=pltpu.VMEM)
HBM = pl.BlockSpec(memory_space=pltpu.HBM)


def rolled(value, shift, axis):
    shift = shift % value.shape[axis]
    return pltpu.roll(value, shift, axis) if shift else value


def rows_out(main, first):
    split = main.reshape(3, 4, ROWS, C)
    group = lax.broadcasted_iota(jnp.int32, (3, ROWS, C), 1) // 2
    out = None
    for q in range(4):
        piece = rolled(split[:, q], 2 * q - first, 1)
        out = piece if out is None else jnp.where(group == q, piece, out)
    return out.reshape(EDGE, C)


def spread(edge, which, to):
    split = edge.reshape(3, ROWS, C)
    pieces = [rolled(split, to - (2 * q + which), 1) for q in range(4)]
    return jnp.stack(pieces, axis=1).reshape(COLS, ROWS, C)


def shifted_row(main, b, before, before_which, after, after_which):
    if b == 1:
        return main
    split = main.reshape(COLS, ROWS, C)
    place = lax.broadcasted_iota(jnp.int32, (COLS, ROWS, C), 1)
    if b == 0:
        moved = jnp.where(place == 0, spread(before, before_which, 0), rolled(split, 1, 1))
    else:
        moved = jnp.where(place == ROWS - 1, spread(after, after_which, ROWS - 1), rolled(split, -1, 1))
    return moved.reshape(MAIN, C)


def column_taps(main):
    zeros = jnp.zeros((ROWS, C), F32)
    return [
        jnp.concatenate([zeros, main[: MAIN - ROWS]], axis=0),
        main,
        jnp.concatenate([main[ROWS:], zeros], axis=0),
    ]


def edge_column_taps(edge):
    place = lax.broadcasted_iota(jnp.int32, (EDGE, C), 0)
    return [
        jnp.where(place < 2, 0.0, rolled(edge, 2, 0)),
        edge,
        jnp.where(place >= EDGE - 2, 0.0, rolled(edge, -2, 0)),
    ]


def edge_pair(top, bottom):
    even = lax.broadcasted_iota(jnp.int32, (EDGE, C), 0) % 2 == 0
    return jnp.where(even, rolled(top, -1, 0), rolled(bottom, 1, 0))


def normed(values, gain):
    factor = lax.rsqrt(jnp.mean(values * values, axis=-1, keepdims=True) + EPSILON)
    v = values * factor * gain
    return v / (1.0 + jnp.exp(-v))


def push_weights(weights, a, step, slot):
    at = step * TILE
    depth = min(TILE, K - at)
    left = weights[a, at : at + depth, 0:TILE]
    right = weights[a, at : at + depth, TILE:C]
    right = jnp.concatenate([right, right], axis=1)
    if depth < TILE:
        empty = jnp.zeros((TILE - depth, TILE), BF16)
        left = jnp.concatenate([left, empty], axis=0)
        right = jnp.concatenate([right, empty], axis=0)
    pltpu.matmul_push_rhs(left, slot, 0)
    pltpu.matmul_push_rhs(right, slot, 1)


def multiply(accumulators, operand, index, step, slot):
    at = step * TILE
    depth = min(TILE, K - at)
    rows = operand[index][:, at : at + depth] if isinstance(operand, list) else operand[index, :, at : at + depth]
    if depth < TILE:
        rows = jnp.concatenate([rows, rows], axis=1)
    for accumulator in accumulators:
        pltpu.matmul_acc_lhs(accumulator, rows, load_staged_rhs=slot)


def popped(accumulators):
    return jnp.concatenate([pltpu.matmul_pop(accumulators[0]), pltpu.matmul_pop(accumulators[1])[:, : C - TILE]], axis=1)


def woven(steps, thunks):
    order, done = [], 0
    for i, step in enumerate(steps):
        order.append(step)
        due = (i + 1) * len(thunks) // len(steps)
        order += thunks[done:due]
        done = due
    return order


class Section:
    def __init__(self, refs, accumulators, live, at_top, at_bottom):
        self.__dict__.update(refs)
        self.live, self.at_top, self.at_bottom = live, at_top, at_bottom
        frames = FRAMES
        self.sums1 = [(accumulators[f], accumulators[frames + f]) for f in range(frames)]
        self.sums2 = [(accumulators[2 * frames + f], accumulators[3 * frames + f]) for f in range(frames)]
        at = 4 * frames
        self.edges1 = [(accumulators[at + i], accumulators[at + 2 + i]) for i in range(2)]
        self.pending = None
        self.slot = 0

    def norm_first(self, f):
        keep = f < self.live
        gain = self.gain1[...]
        values = jnp.where(keep, self.x[f].astype(F32), 0.0)
        self.window1[f + 2, 0:MAIN] = normed(values, gain).astype(BF16)

    def norm_first_halo(self, f):
        keep = f < self.live
        gain = self.gain1[...]
        top = jnp.where(keep & jnp.logical_not(self.at_top), self.tops[f].astype(F32), 0.0)
        bottom = jnp.where(keep & jnp.logical_not(self.at_bottom), self.bottoms[f].astype(F32), 0.0)
        values = jnp.concatenate([top, bottom], axis=0)
        self.window1[f + 2, MAIN : MAIN + 2 * EDGE] = normed(values, gain).astype(BF16)

    def build_first_edges(self, g):
        main = self.window1[g, 0:MAIN].astype(F32)
        halo = self.window1[g, MAIN : MAIN + 2 * EDGE].astype(F32)
        top, bottom = halo[:EDGE], halo[EDGE:]
        even = lax.broadcasted_iota(jnp.int32, (EDGE, C), 0) % 2 == 0
        self.edge_rows[g, 0] = jnp.where(even, top, rows_out(main, 6))
        self.edge_rows[g, 1] = edge_pair(top, bottom)
        self.edge_rows[g, 2] = jnp.where(even, rows_out(main, 0), bottom)

    def build_first_pair(self, g, b):
        taps = [edge_column_taps(self.edge_rows[g + i, b]) for i in range(2)]
        for c in range(3):
            at = (3 * b + c) * C
            rows = jnp.concatenate([taps[0][c], taps[1][c]], axis=0)
            self.edges[g, :, at : at + C] = rows.astype(BF16)

    def build_first(self, g, b):
        main = self.window1[g, 0:MAIN].astype(F32)
        halo = self.window1[g, MAIN : MAIN + 2 * EDGE].astype(F32)
        self.build(self.operand1, g, b, main, halo[:EDGE], 1, halo[EDGE:], 0)

    def build_second(self, g, b):
        main = self.window2[g].astype(F32)
        edge = self.hidden_edges[g]
        self.build(self.operand2, g, b, main, edge, 0, edge, 1)

    def build(self, operand, g, b, main, before, before_which, after, after_which):
        rows = shifted_row(main, b, before, before_which, after, after_which)
        for c, taps in enumerate(column_taps(rows)):
            at = (3 * b + c) * C
            operand[g, :, at : at + C] = taps.astype(BF16)

    def first_thunks(self, pair, cached=False):
        out = []
        for g in (pair, pair + 1):
            if not cached:
                out += [lambda f=g - 2: self.norm_first(f), lambda f=g - 2: self.norm_first_halo(f)]
        for g in (pair, pair + 1):
            out += [lambda g=g: self.build_first_edges(g)]
            out += [lambda g=g, b=b: self.build_first(g, b) for b in range(3)]
        starts = [pair] if pair == 0 else [pair - 1, pair]
        out += [lambda g=g, b=b: self.build_first_pair(g, b) for g in starts for b in range(3)]
        return out

    def second_thunks(self, pair, cached=False):
        out = []
        if not cached:
            out += [lambda f=f: self.norm_second(f) for f in (pair - 2, pair - 1)]
            out += [lambda i=pair // 2 - 1: self.norm_second_edges(i)]
        out += [lambda g=g, b=b: self.build_second(g, b) for g in (pair, pair + 1) for b in range(3)]
        return out

    def norm_second(self, f):
        hidden = popped(self.sums1[f]) + self.bias1[...]
        if self.early1 is not None and f < 2:
            hidden = hidden + self.early1[f]
        hidden = jnp.where(f < self.live, hidden, 0.0)
        self.window2[f + 2] = normed(hidden, self.gain2[...]).astype(BF16)

    def norm_second_edges(self, i):
        hidden = popped(self.edges1[i]) + self.bias1[...]
        if self.early1 is not None and i == 0:
            hidden = hidden + self.early_edges[...]
        place = lax.broadcasted_iota(jnp.int32, (2 * EDGE, C), 0)
        outside = ((place % 2 == 0) & self.at_top) | ((place % 2 == 1) & self.at_bottom)
        hidden = jnp.where(outside, 0.0, hidden)
        values = normed(hidden, self.gain2[...]).astype(BF16).astype(F32)
        for j in range(2):
            f = 2 * i + j
            self.hidden_edges[f + 2] = jnp.where(f < self.live, values[j * EDGE : (j + 1) * EDGE], 0.0)

    def phase(self, conv, pair):
        weights = (self.weights1, self.weights2)[conv]
        operand = (self.operand1, self.operand2)[conv]
        sums = (self.sums1, self.sums2)[conv]
        steps = []
        for a in range(3):
            work = [(sums[g - a], operand, g) for g in (pair, pair + 1) if 0 <= g - a < FRAMES]
            if conv == 0:
                for i in range(2):
                    if pair <= 2 * i + a + 1 < pair + 2:
                        work.append((self.edges1[i], self.edges, 2 * i + a))
            if work:
                steps += [(conv, a, step, weights, work) for step in range(STEPS)]
        return steps

    def run(self, order):
        steps = [entry for entry in order if isinstance(entry, tuple)]
        ready = set()

        def push(i):
            conv, a, step, weights, _ = steps[i]
            if (conv, a) not in ready:
                ready.add((conv, a))
                self.wait_weights(conv, a)
            push_weights(weights, a, step, i % 2)

        i = 0
        for entry in order:
            if not isinstance(entry, tuple):
                entry()
                continue
            if i == 0:
                push(0)
            if i + 1 < len(steps):
                push(i + 1)
            _, _, step, _, work = entry
            for n, (accumulators, operand, g) in enumerate(work):
                multiply(accumulators, operand, g, step, i % 2 if n == 0 else None)
            i += 1


def pack_kernel(x, first, second, up, down):
    for source, start in ((x, 0), (first, 4), (second, 6)):
        for f in range(source.shape[0]):
            main = source[f].astype(F32)
            up[start + f] = rows_out(main, 0).astype(BF16)
            down[start + f] = rows_out(main, 6).astype(BF16)


SCRATCH = dict(
    window1=pltpu.VMEM((FRAMES + 2, MAIN + 2 * EDGE, C), BF16),
    window2=pltpu.VMEM((FRAMES + 2, MAIN, C), BF16),
    edge_rows=pltpu.VMEM((FRAMES + 2, 3, EDGE, C), F32),
    hidden_edges=pltpu.VMEM((FRAMES + 2, EDGE, C), F32),
    operand1=pltpu.VMEM((FRAMES + 2, MAIN, K), BF16),
    edges=pltpu.VMEM((FRAMES + 1, 2 * EDGE, K), BF16),
    operand2=pltpu.VMEM((FRAMES + 2, MAIN, K), BF16),
    weights1=pltpu.VMEM((3, K, C), BF16),
    weights2=pltpu.VMEM((3, K, C), BF16),
    result=pltpu.VMEM((FRAMES, MAIN, C), BF16),
)
VECTORS = ("bias1", "gain1", "bias2", "gain2")
BLOCKS = dict(x=(FRAMES, MAIN, C), first=(2, MAIN, C), second=(2, MAIN, C), incoming=(FRAMES, MAIN, C))


def tick_kernel(tick, inputs, outputs, scratch, *refs):
    names = list(inputs) + list(outputs) + list(scratch)
    given = dict(zip(names, refs))
    accumulators = given.pop("accumulators", None)
    sems = given["sems"]
    copies = {}
    for name in inputs:
        if name + "_hbm" == name or not name.endswith("_hbm"):
            continue
        inner = name[:-4]
        if inner in ("weights1", "weights2"):
            continue
        copies[inner] = pltpu.make_async_copy(given[name], given[inner], sems.at[len(copies)])
    count = len(copies)
    for conv, inner in enumerate(("weights1", "weights2")):
        for a in range(3):
            copies[conv, a] = pltpu.make_async_copy(
                given[inner + "_hbm"].at[a], given[inner].at[a], sems.at[count + 3 * conv + a]
            )
    for copy in copies.values():
        copy.start()
    segment = lax.axis_index("segment")
    strip = lax.axis_index("strip")
    copies.pop("counts").wait()
    live = given["counts"][7 - segment + tick]
    at_top = strip == 0
    at_bottom = strip == lax.axis_size("strip") - 1

    def body(*accumulators):
        fields = dict(given)
        fields.setdefault("early1", None)
        work = Section(fields, accumulators, live, at_top, at_bottom)
        work.wait_weights = lambda conv, a: copies[conv, a].wait()
        for name in copies:
            if isinstance(name, str):
                copies[name].wait()
        work.window1[0:2, 0:MAIN] = work.first[...]
        work.window2[0:2] = work.second[...]
        if tick == 0:
            none = jnp.zeros((2, EDGE, C), BF16)
            work.window1[0:2, MAIN : MAIN + EDGE] = jnp.where(at_top, none, work.tops[4:6])
            work.window1[0:2, MAIN + EDGE : MAIN + 2 * EDGE] = jnp.where(at_bottom, none, work.bottoms[4:6])
            for g in range(2):
                work.hidden_edges[g] = edge_pair(
                    jnp.where(at_top, 0.0, work.tops[6 + g].astype(F32)),
                    jnp.where(at_bottom, 0.0, work.bottoms[6 + g].astype(F32)),
                )
        else:
            work.window1[0:2, MAIN : MAIN + 2 * EDGE] = work.first_halo[...]
            for g in range(2):
                work.hidden_edges[g] = work.second_edge[g].astype(F32)
        order = work.first_thunks(0, cached=True)
        order += woven(work.phase(0, 0), work.first_thunks(2))
        order += woven(work.phase(0, 2), work.first_thunks(4) + work.second_thunks(0, cached=True))
        order += woven(work.phase(0, 4), work.second_thunks(2))
        order += woven(work.phase(1, 0), work.second_thunks(4))
        order += work.phase(1, 2) + work.phase(1, 4)
        work.run(order)
        bias2 = work.bias2[...]
        for f in range(FRAMES):
            result = popped(work.sums2[f]) + bias2 + work.x[f].astype(F32)
            result = jnp.where(f < live, result, 0.0).astype(BF16)
            work.result[f] = result
            if tick == 0:
                last = segment == lax.axis_size("segment") - 1
                passed = jnp.where(last, work.incoming[f].astype(F32), result.astype(F32))
                work.send[f] = passed.astype(BF16)
                work.send_up[f] = rows_out(passed, 0).astype(BF16)
                work.send_down[f] = rows_out(passed, 6).astype(BF16)

    shapes = [MAIN] * (4 * FRAMES) + [2 * EDGE] * 4
    units = ([0] * FRAMES + [1] * FRAMES) * 2 + [0, 0, 1, 1]
    pl.run_scoped(body, *[pltpu.ACC(unit)((rows, TILE), F32) for unit, rows in zip(units, shapes)])
    copy = pltpu.make_async_copy(given["result"], given["whole"].at[tick], sems.at[0])
    copy.start()
    for i in range(2):
        given["first_next"][i] = given["window1"][live + i, 0:MAIN]
        given["second_next"][i] = given["window2"][live + i]
        if tick == 0:
            given["halo_next"][i] = given["window1"][live + i, MAIN : MAIN + 2 * EDGE]
            given["edge_next"][i] = given["hidden_edges"][live + i].astype(BF16)
    copy.wait()


def shape(*dims):
    return jax.ShapeDtypeStruct(dims, BF16)


def run_tick(tick, operands, out_shapes):
    inputs = list(operands)
    outputs = list(out_shapes)
    scratch = dict(SCRATCH)
    for name in inputs:
        inner = name[:-4]
        if name.endswith("_hbm") and inner in BLOCKS:
            scratch[inner] = pltpu.VMEM(BLOCKS[inner], BF16)
        if name == "counts_hbm":
            scratch["counts"] = pltpu.SMEM((9,), jnp.int32)
        if name.endswith("_hbm") and inner in VECTORS:
            scratch[inner] = pltpu.VMEM((1, C), F32)
    scratch["sems"] = pltpu.SemaphoreType.DMA((16,))
    places = [HBM if n.endswith("_hbm") or n == "base" else VMEM for n in inputs]
    operands = {
        n: pltpu.with_memory_space_constraint(v, pltpu.HBM) if n.endswith("_hbm") else v for n, v in operands.items()
    }
    aliases = {inputs.index("base"): outputs.index("whole")} if "base" in inputs else {}
    return pl.pallas_call(
        lambda *refs: tick_kernel(tick, inputs, outputs, scratch, *refs),
        out_shape=list(out_shapes.values()),
        in_specs=places,
        out_specs=[HBM if n == "whole" else VMEM for n in outputs],
        input_output_aliases=aliases,
        scratch_shapes=list(scratch.values()),
        compiler_params=pltpu.CompilerParams(vmem_limit_bytes=48 << 20),
        name=f"tick{tick}",
    )(*operands.values())


def flat(array):
    frames = array.shape[0]
    return array.transpose(0, 2, 1, 3).reshape(frames, MAIN, C)


def unflat(array):
    frames = array.shape[0]
    return array.reshape(frames, COLS, ROWS, C).transpose(0, 2, 1, 3)


def on_device(
    held_blocks,
    incoming,
    frame_counts,
    first_cache,
    second_cache,
    first_kernel,
    first_bias,
    first_gain,
    second_kernel,
    second_bias,
    second_gain,
):
    segments = lax.axis_size("segment")
    strips = lax.axis_size("strip")
    x = flat(held_blocks[0])
    fresh = flat(incoming[0])
    first = flat(first_cache[0])
    second = flat(second_cache[0])
    params = dict(
        bias1_hbm=first_bias,
        gain1_hbm=first_gain,
        bias2_hbm=second_bias,
        gain2_hbm=second_gain,
        weights1_hbm=first_kernel[0].reshape(3, K, C),
        weights2_hbm=second_kernel[0].reshape(3, K, C),
    )
    up, down = pl.pallas_call(
        pack_kernel, out_shape=[shape(8, EDGE, C)] * 2, in_specs=[VMEM] * 3, out_specs=[VMEM] * 2, name="pack"
    )(x, first, second)
    forward = [(i, (i + 1) % strips) for i in range(strips)]
    backward = [(j, i) for i, j in forward]
    tops = lax.ppermute(down, "strip", forward)
    bottoms = lax.ppermute(up, "strip", backward)
    whole, send, send_up, send_down, first, first_halo, second, second_edge = run_tick(
        0,
        dict(
            counts_hbm=frame_counts,
            tops=tops,
            bottoms=bottoms,
            x_hbm=x,
            first_hbm=first,
            second_hbm=second,
            incoming_hbm=fresh,
            **params,
        ),
        dict(
            whole=shape(2, FRAMES, MAIN, C),
            send=shape(FRAMES, MAIN, C),
            send_up=shape(FRAMES, EDGE, C),
            send_down=shape(FRAMES, EDGE, C),
            first_next=shape(2, MAIN, C),
            halo_next=shape(2, 2 * EDGE, C),
            second_next=shape(2, MAIN, C),
            edge_next=shape(2, EDGE, C),
        ),
    )

    def pairs(step):
        return [
            (s * strips + k, (s + 1) % segments * strips + (k + step) % strips)
            for s in range(segments)
            for k in range(strips)
        ]

    axes = ("segment", "strip")
    tops = lax.ppermute(send_down, axes, pairs(1))
    bottoms = lax.ppermute(send_up, axes, pairs(-1))
    x = lax.ppermute(send, axes, pairs(0))
    whole, first, second = run_tick(
        1,
        dict(
            counts_hbm=frame_counts,
            x=x,
            tops=tops,
            bottoms=bottoms,
            first=first,
            first_halo=first_halo,
            second=second,
            second_edge=second_edge,
            base=whole,
            **params,
        ),
        dict(whole=shape(2, FRAMES, MAIN, C), first_next=shape(2, MAIN, C), second_next=shape(2, MAIN, C)),
    )
    return (
        unflat(whole.reshape(2 * FRAMES, MAIN, C)).reshape(2, 1, FRAMES, ROWS, COLS, C),
        unflat(first)[None],
        unflat(second)[None],
    )


def solution(mesh):
    return jax.shard_map(
        on_device,
        mesh=mesh,
        in_specs=(
            P("segment", None, "strip", None, None),
            P(None, None, "strip", None, None),
            P(),
            P("segment", None, "strip", None, None),
            P("segment", None, "strip", None, None),
            P("segment", None, None, None, None, None),
            P("segment", None),
            P("segment", None),
            P("segment", None, None, None, None, None),
            P("segment", None),
            P("segment", None),
        ),
        out_specs=(
            P(None, "segment", None, "strip", None, None),
            P("segment", None, "strip", None, None),
            P("segment", None, "strip", None, None),
        ),
        check_vma=False,
    )
```

```python
import jax
import jax.numpy as jnp
from jax import lax
from jax.experimental import pallas as pl
from jax.experimental.pallas import tpu as pltpu
from jax.sharding import PartitionSpec as P

EPSILON = 1e-06
C = 384
FRAMES = 4
COLS = 12
ROWS = 8
MAIN = COLS * ROWS
EDGE = COLS * 2
TAPS = 9
K = TAPS * C
TILE = 256
STEPS = -(-K // TILE)
BF16 = jnp.bfloat16
F32 = jnp.float32
VMEM = pl.BlockSpec(memory_space=pltpu.VMEM)
HBM = pl.BlockSpec(memory_space=pltpu.HBM)


def rolled(value, shift, axis):
    shift = shift % value.shape[axis]
    return pltpu.roll(value, shift, axis) if shift else value


def rows_out(main, first):
    split = main.reshape(3, 4, ROWS, C)
    group = lax.broadcasted_iota(jnp.int32, (3, ROWS, C), 1) // 2
    out = None
    for q in range(4):
        piece = rolled(split[:, q], 2 * q - first, 1)
        out = piece if out is None else jnp.where(group == q, piece, out)
    return out.reshape(EDGE, C)


def spread(edge, which, to):
    split = edge.reshape(3, ROWS, C)
    pieces = [rolled(split, to - (2 * q + which), 1) for q in range(4)]
    return jnp.stack(pieces, axis=1).reshape(COLS, ROWS, C)


def shifted_row(main, b, before, before_which, after, after_which):
    if b == 1:
        return main
    split = main.reshape(COLS, ROWS, C)
    place = lax.broadcasted_iota(jnp.int32, (COLS, ROWS, C), 1)
    if b == 0:
        moved = jnp.where(place == 0, spread(before, before_which, 0), rolled(split, 1, 1))
    else:
        moved = jnp.where(place == ROWS - 1, spread(after, after_which, ROWS - 1), rolled(split, -1, 1))
    return moved.reshape(MAIN, C)


def column_taps(main):
    zeros = jnp.zeros((ROWS, C), F32)
    return [
        jnp.concatenate([zeros, main[: MAIN - ROWS]], axis=0),
        main,
        jnp.concatenate([main[ROWS:], zeros], axis=0),
    ]


def edge_column_taps(edge):
    place = lax.broadcasted_iota(jnp.int32, (EDGE, C), 0)
    return [
        jnp.where(place < 2, 0.0, rolled(edge, 2, 0)),
        edge,
        jnp.where(place >= EDGE - 2, 0.0, rolled(edge, -2, 0)),
    ]


def edge_pair(top, bottom):
    even = lax.broadcasted_iota(jnp.int32, (EDGE, C), 0) % 2 == 0
    return jnp.where(even, rolled(top, -1, 0), rolled(bottom, 1, 0))


def normed(values, gain):
    factor = lax.rsqrt(jnp.mean(values * values, axis=-1, keepdims=True) + EPSILON)
    v = values * factor * gain
    return v / (1.0 + jnp.exp(-v))


def push_weights(weights, a, step, slot):
    at = step * TILE
    depth = min(TILE, K - at)
    left = weights[a, at : at + depth, 0:TILE]
    right = weights[a, at : at + depth, TILE:C]
    right = jnp.concatenate([right, right], axis=1)
    if depth < TILE:
        empty = jnp.zeros((TILE - depth, TILE), BF16)
        left = jnp.concatenate([left, empty], axis=0)
        right = jnp.concatenate([right, empty], axis=0)
    pltpu.matmul_push_rhs(left, slot, 0)
    pltpu.matmul_push_rhs(right, slot, 1)


def multiply(accumulators, operand, index, step, slot):
    at = step * TILE
    depth = min(TILE, K - at)
    rows = operand[index][:, at : at + depth] if isinstance(operand, list) else operand[index, :, at : at + depth]
    if depth < TILE:
        rows = jnp.concatenate([rows, rows], axis=1)
    for accumulator in accumulators:
        pltpu.matmul_acc_lhs(accumulator, rows, load_staged_rhs=slot)


def popped(accumulators):
    return jnp.concatenate([pltpu.matmul_pop(accumulators[0]), pltpu.matmul_pop(accumulators[1])[:, : C - TILE]], axis=1)


def woven(steps, thunks):
    order, done = [], 0
    for i, step in enumerate(steps):
        order.append(step)
        due = (i + 1) * len(thunks) // len(steps)
        order += thunks[done:due]
        done = due
    return order


class Section:
    def __init__(self, refs, accumulators, live, even, at_top, at_bottom):
        self.__dict__.update(refs)
        self.live, self.even, self.at_top, self.at_bottom = live, even, at_top, at_bottom
        frames = FRAMES
        self.sums1 = [(accumulators[f], accumulators[frames + f]) for f in range(frames)]
        self.sums2 = [(accumulators[2 * frames + f], accumulators[3 * frames + f]) for f in range(frames)]
        at = 4 * frames
        self.edges1 = [(accumulators[at + i], accumulators[at + 2 + i]) for i in range(2)]

    def halo(self, f):
        near, far = self.near[f].astype(F32), self.far[f].astype(F32)
        top = jnp.where(self.at_top, 0.0, jnp.where(self.even, far, near))
        bottom = jnp.where(self.at_bottom, 0.0, jnp.where(self.even, near, far))
        return top, bottom

    def norm_first(self, f):
        keep = f < self.live
        gain = self.gain1[...]
        values = jnp.where(keep, self.x[f].astype(F32), 0.0)
        self.window1[f + 2, 0:MAIN] = normed(values, gain).astype(BF16)

    def norm_first_halo(self, f):
        keep = f < self.live
        gain = self.gain1[...]
        top, bottom = (jnp.where(keep, rows, 0.0) for rows in self.halo(f))
        values = jnp.concatenate([top, bottom], axis=0)
        self.window1[f + 2, MAIN : MAIN + 2 * EDGE] = normed(values, gain).astype(BF16)

    def build_first_edges(self, g):
        main = self.window1[g, 0:MAIN].astype(F32)
        halo = self.window1[g, MAIN : MAIN + 2 * EDGE].astype(F32)
        top, bottom = halo[:EDGE], halo[EDGE:]
        even = lax.broadcasted_iota(jnp.int32, (EDGE, C), 0) % 2 == 0
        self.edge_rows[g, 0] = jnp.where(even, top, rows_out(main, 6))
        self.edge_rows[g, 1] = edge_pair(top, bottom)
        self.edge_rows[g, 2] = jnp.where(even, rows_out(main, 0), bottom)

    def build_first_pair(self, g, b):
        taps = [edge_column_taps(self.edge_rows[g + i, b]) for i in range(2)]
        for c in range(3):
            at = (3 * b + c) * C
            rows = jnp.concatenate([taps[0][c], taps[1][c]], axis=0)
            self.edges[g, :, at : at + C] = rows.astype(BF16)

    def build_first(self, g, b):
        main = self.window1[g, 0:MAIN].astype(F32)
        halo = self.window1[g, MAIN : MAIN + 2 * EDGE].astype(F32)
        self.build(self.operand1, g, b, main, halo[:EDGE], 1, halo[EDGE:], 0)

    def build_second(self, g, b):
        main = self.window2[g].astype(F32)
        edge = self.hidden_edges[g]
        self.build(self.operand2, g, b, main, edge, 0, edge, 1)

    def build(self, operand, g, b, main, before, before_which, after, after_which):
        rows = shifted_row(main, b, before, before_which, after, after_which)
        for c, taps in enumerate(column_taps(rows)):
            at = (3 * b + c) * C
            operand[g, :, at : at + C] = taps.astype(BF16)

    def first_thunks(self, pair, cached=False):
        out = []
        for g in (pair, pair + 1):
            if not cached:
                out += [lambda f=g - 2: self.norm_first(f), lambda f=g - 2: self.norm_first_halo(f)]
        for g in (pair, pair + 1):
            out += [lambda g=g: self.build_first_edges(g)]
            out += [lambda g=g, b=b: self.build_first(g, b) for b in range(3)]
        starts = [pair] if pair == 0 else [pair - 1, pair]
        out += [lambda g=g, b=b: self.build_first_pair(g, b) for g in starts for b in range(3)]
        return out

    def second_thunks(self, pair, cached=False):
        out = []
        if not cached:
            out += [lambda f=f: self.norm_second(f) for f in (pair - 2, pair - 1)]
            out += [lambda i=pair // 2 - 1: self.norm_second_edges(i)]
        out += [lambda g=g, b=b: self.build_second(g, b) for g in (pair, pair + 1) for b in range(3)]
        return out

    def norm_second(self, f):
        hidden = popped(self.sums1[f]) + self.bias1[...]
        if self.early1 is not None and f < 2:
            hidden = hidden + self.early1[f]
        hidden = jnp.where(f < self.live, hidden, 0.0)
        self.window2[f + 2] = normed(hidden, self.gain2[...]).astype(BF16)

    def norm_second_edges(self, i):
        hidden = popped(self.edges1[i]) + self.bias1[...]
        if self.early1 is not None and i == 0:
            hidden = hidden + self.early_edges[...]
        place = lax.broadcasted_iota(jnp.int32, (2 * EDGE, C), 0)
        outside = ((place % 2 == 0) & self.at_top) | ((place % 2 == 1) & self.at_bottom)
        hidden = jnp.where(outside, 0.0, hidden)
        values = normed(hidden, self.gain2[...]).astype(BF16).astype(F32)
        for j in range(2):
            f = 2 * i + j
            self.hidden_edges[f + 2] = jnp.where(f < self.live, values[j * EDGE : (j + 1) * EDGE], 0.0)

    def phase(self, conv, pair):
        weights = (self.weights1, self.weights2)[conv]
        operand = (self.operand1, self.operand2)[conv]
        sums = (self.sums1, self.sums2)[conv]
        steps = []
        for a in range(3):
            work = [(sums[g - a], operand, g) for g in (pair, pair + 1) if 0 <= g - a < FRAMES]
            if conv == 0:
                for i in range(2):
                    if pair <= 2 * i + a + 1 < pair + 2:
                        work.append((self.edges1[i], self.edges, 2 * i + a))
            if work:
                steps += [(conv, a, step, weights, work) for step in range(STEPS)]
        return steps

    def run(self, order):
        steps = [entry for entry in order if isinstance(entry, tuple)]

        def push(i):
            _, a, step, weights, _ = steps[i]
            push_weights(weights, a, step, i % 2)

        i = 0
        for entry in order:
            if not isinstance(entry, tuple):
                entry()
                continue
            if i == 0:
                push(0)
            if i + 1 < len(steps):
                push(i + 1)
            _, _, step, _, work = entry
            for n, (accumulators, operand, g) in enumerate(work):
                multiply(accumulators, operand, g, step, i % 2 if n == 0 else None)
            i += 1


def load_kernel(first, second, first_out, second_out, sems):
    copies = [
        pltpu.make_async_copy(source.at[a], target.at[a], sems.at[i, a])
        for i, (source, target) in enumerate(((first, first_out), (second, second_out)))
        for a in range(3)
    ]
    for copy in copies:
        copy.start()
    for copy in copies:
        copy.wait()


def edges_out(main, even, near, far, f):
    upper, lower = rows_out(main, 0), rows_out(main, 6)
    near[f] = jnp.where(even, lower, upper).astype(BF16)
    far[f] = jnp.where(even, upper, lower).astype(BF16)


def pack_kernel(x, first, second, near, far):
    even = lax.axis_index("strip") % 2 == 0
    for source, start in ((x, 0), (first, 4), (second, 6)):
        for f in range(source.shape[0]):
            edges_out(source[f].astype(F32), even, near, far, start + f)


SCRATCH = dict(
    window1=pltpu.VMEM((FRAMES + 2, MAIN + 2 * EDGE, C), BF16),
    window2=pltpu.VMEM((FRAMES + 2, MAIN, C), BF16),
    edge_rows=pltpu.VMEM((FRAMES + 2, 3, EDGE, C), F32),
    hidden_edges=pltpu.VMEM((FRAMES + 2, EDGE, C), F32),
    operand1=pltpu.VMEM((FRAMES + 2, MAIN, K), BF16),
    edges=pltpu.VMEM((FRAMES + 1, 2 * EDGE, K), BF16),
    operand2=pltpu.VMEM((FRAMES + 2, MAIN, K), BF16),
    result=pltpu.VMEM((FRAMES, MAIN, C), BF16),
)
VECTORS = ("bias1", "gain1", "bias2", "gain2")
BLOCKS = dict(x=(FRAMES, MAIN, C), first=(2, MAIN, C), second=(2, MAIN, C), incoming=(FRAMES, MAIN, C))


def tick_kernel(tick, inputs, outputs, scratch, *refs):
    names = list(inputs) + list(outputs) + list(scratch)
    given = dict(zip(names, refs))
    accumulators = given.pop("accumulators", None)
    sems = given["sems"]
    copies = {}
    for name in inputs:
        if name + "_hbm" == name or not name.endswith("_hbm"):
            continue
        inner = name[:-4]
        copies[inner] = pltpu.make_async_copy(given[name], given[inner], sems.at[len(copies)])
    for copy in copies.values():
        copy.start()
    segment = lax.axis_index("segment")
    strip = lax.axis_index("strip")
    copies.pop("counts").wait()
    live = given["counts"][7 - segment + tick]
    at_top = strip == 0
    at_bottom = strip == lax.axis_size("strip") - 1

    def body(*accumulators):
        fields = dict(given)
        fields.setdefault("early1", None)
        work = Section(fields, accumulators, live, strip % 2 == 0, at_top, at_bottom)
        for copy in copies.values():
            copy.wait()
        work.window1[0:2, 0:MAIN] = work.first[...]
        work.window2[0:2] = work.second[...]
        if tick == 0:
            for g in range(2):
                rows = jnp.concatenate(work.halo(4 + g), axis=0)
                work.window1[g, MAIN : MAIN + 2 * EDGE] = rows.astype(BF16)
                work.hidden_edges[g] = edge_pair(*work.halo(6 + g))
        else:
            work.window1[0:2, MAIN : MAIN + 2 * EDGE] = work.first_halo[...]
            for g in range(2):
                work.hidden_edges[g] = work.second_edge[g].astype(F32)
        order = work.first_thunks(0, cached=True)
        order += woven(work.phase(0, 0), work.first_thunks(2))
        order += woven(work.phase(0, 2), work.first_thunks(4) + work.second_thunks(0, cached=True))
        order += woven(work.phase(0, 4), work.second_thunks(2))
        order += woven(work.phase(1, 0), work.second_thunks(4))
        order += work.phase(1, 2) + work.phase(1, 4)
        work.run(order)
        bias2 = work.bias2[...]
        for f in range(FRAMES):
            result = popped(work.sums2[f]) + bias2 + work.x[f].astype(F32)
            result = jnp.where(f < live, result, 0.0).astype(BF16)
            work.result[f] = result
            if tick == 0:
                last = segment == lax.axis_size("segment") - 1
                passed = jnp.where(last, work.incoming[f].astype(F32), result.astype(F32))
                work.send[f] = passed.astype(BF16)
                edges_out(passed, work.even, work.send_near, work.send_far, f)

    shapes = [MAIN] * (4 * FRAMES) + [2 * EDGE] * 4
    units = ([0] * FRAMES + [1] * FRAMES) * 2 + [0, 0, 1, 1]
    pl.run_scoped(body, *[pltpu.ACC(unit)((rows, TILE), F32) for unit, rows in zip(units, shapes)])
    copy = pltpu.make_async_copy(given["result"], given["whole"].at[tick], sems.at[0])
    copy.start()
    for i in range(2):
        given["first_next"][i] = given["window1"][live + i, 0:MAIN]
        given["second_next"][i] = given["window2"][live + i]
        if tick == 0:
            given["halo_next"][i] = given["window1"][live + i, MAIN : MAIN + 2 * EDGE]
            given["edge_next"][i] = given["hidden_edges"][live + i].astype(BF16)
    copy.wait()


def shape(*dims):
    return jax.ShapeDtypeStruct(dims, BF16)


def run_tick(tick, operands, out_shapes):
    inputs = list(operands)
    outputs = list(out_shapes)
    scratch = dict(SCRATCH)
    for name in inputs:
        inner = name[:-4]
        if name.endswith("_hbm") and inner in BLOCKS:
            scratch[inner] = pltpu.VMEM(BLOCKS[inner], BF16)
        if name == "counts_hbm":
            scratch["counts"] = pltpu.SMEM((9,), jnp.int32)
        if name.endswith("_hbm") and inner in VECTORS:
            scratch[inner] = pltpu.VMEM((1, C), F32)
    scratch["sems"] = pltpu.SemaphoreType.DMA((16,))
    places = [HBM if n.endswith("_hbm") or n == "base" else VMEM for n in inputs]
    operands = {
        n: pltpu.with_memory_space_constraint(v, pltpu.HBM) if n.endswith("_hbm") else v for n, v in operands.items()
    }
    aliases = {inputs.index("base"): outputs.index("whole")} if "base" in inputs else {}
    return pl.pallas_call(
        lambda *refs: tick_kernel(tick, inputs, outputs, scratch, *refs),
        out_shape=list(out_shapes.values()),
        in_specs=places,
        out_specs=[HBM if n == "whole" else VMEM for n in outputs],
        input_output_aliases=aliases,
        scratch_shapes=list(scratch.values()),
        compiler_params=pltpu.CompilerParams(vmem_limit_bytes=24 << 20),
        name=f"tick{tick}",
    )(*operands.values())


def flat(array):
    frames = array.shape[0]
    return array.transpose(0, 2, 1, 3).reshape(frames, MAIN, C)


def unflat(array):
    frames = array.shape[0]
    return array.reshape(frames, COLS, ROWS, C).transpose(0, 2, 1, 3)


def on_device(
    held_blocks,
    incoming,
    frame_counts,
    first_cache,
    second_cache,
    first_kernel,
    first_bias,
    first_gain,
    second_kernel,
    second_bias,
    second_gain,
):
    segments = lax.axis_size("segment")
    strips = lax.axis_size("strip")
    x = flat(held_blocks[0])
    fresh = flat(incoming[0])
    first = flat(first_cache[0])
    second = flat(second_cache[0])
    weights1, weights2 = pl.pallas_call(
        load_kernel,
        out_shape=[pltpu.VMEM((3, K, C), BF16)] * 2,
        in_specs=[HBM] * 2,
        out_specs=[VMEM] * 2,
        scratch_shapes=[pltpu.SemaphoreType.DMA((2, 3))],
        compiler_params=pltpu.CompilerParams(vmem_limit_bytes=1 << 20),
        cost_estimate=pl.CostEstimate(flops=0, bytes_accessed=4 * 3 * K * C, transcendentals=0),
        name="load",
    )(
        *(
            pltpu.with_memory_space_constraint(kernel[0].reshape(3, K, C), pltpu.HBM)
            for kernel in (first_kernel, second_kernel)
        )
    )
    params = dict(
        bias1_hbm=first_bias,
        gain1_hbm=first_gain,
        bias2_hbm=second_bias,
        gain2_hbm=second_gain,
        weights1=weights1,
        weights2=weights2,
    )
    near, far = pl.pallas_call(
        pack_kernel, out_shape=[shape(8, EDGE, C)] * 2, in_specs=[VMEM] * 3, out_specs=[VMEM] * 2, name="pack"
    )(x, first, second)
    swaps = [
        [(i, i ^ 1) for i in range(strips)],
        [(i, (((i + 1) ^ 1) - 1) % strips) for i in range(strips)],
    ]
    near, far = (lax.ppermute(rows, "strip", swap) for rows, swap in zip((near, far), swaps))
    whole, send, send_near, send_far, first, first_halo, second, second_edge = run_tick(
        0,
        dict(
            counts_hbm=frame_counts,
            near=near,
            far=far,
            x_hbm=x,
            first_hbm=first,
            second_hbm=second,
            incoming_hbm=fresh,
            **params,
        ),
        dict(
            whole=shape(2, FRAMES, MAIN, C),
            send=shape(FRAMES, MAIN, C),
            send_near=shape(FRAMES, EDGE, C),
            send_far=shape(FRAMES, EDGE, C),
            first_next=shape(2, MAIN, C),
            halo_next=shape(2, 2 * EDGE, C),
            second_next=shape(2, MAIN, C),
            edge_next=shape(2, EDGE, C),
        ),
    )

    def onward(rows, swap):
        pairs = [(s * strips + i, (s + 1) % segments * strips + j) for s in range(segments) for i, j in swap]
        return lax.ppermute(rows, ("segment", "strip"), pairs)

    x = onward(send, [(i, i) for i in range(strips)])
    near, far = (onward(rows, swap) for rows, swap in zip((send_near, send_far), swaps))
    whole, first, second = run_tick(
        1,
        dict(
            counts_hbm=frame_counts,
            x=x,
            near=near,
            far=far,
            first=first,
            first_halo=first_halo,
            second=second,
            second_edge=second_edge,
            base=whole,
            **params,
        ),
        dict(whole=shape(2, FRAMES, MAIN, C), first_next=shape(2, MAIN, C), second_next=shape(2, MAIN, C)),
    )
    return (
        unflat(whole.reshape(2 * FRAMES, MAIN, C)).reshape(2, 1, FRAMES, ROWS, COLS, C),
        unflat(first)[None],
        unflat(second)[None],
    )


def solution(mesh):
    return jax.shard_map(
        on_device,
        mesh=mesh,
        in_specs=(
            P("segment", None, "strip", None, None),
            P(None, None, "strip", None, None),
            P(),
            P("segment", None, "strip", None, None),
            P("segment", None, "strip", None, None),
            P("segment", None, None, None, None, None),
            P("segment", None),
            P("segment", None),
            P("segment", None, None, None, None, None),
            P("segment", None),
            P("segment", None),
        ),
        out_specs=(
            P(None, "segment", None, "strip", None, None),
            P("segment", None, "strip", None, None),
            P("segment", None, "strip", None, None),
        ),
        check_vma=False,
    )
```

```python
import jax
import jax.numpy as jnp
from jax import lax
from jax.experimental import pallas as pl
from jax.experimental.pallas import tpu as pltpu
from jax.sharding import PartitionSpec as P

EPSILON = 1e-06
C = 384
FRAMES = 4
COLS = 12
ROWS = 8
MAIN = COLS * ROWS
EDGE = COLS * 2
TAPS = 9
K = TAPS * C
TILE = 256
STEPS = -(-K // TILE)
BF16 = jnp.bfloat16
F32 = jnp.float32
VMEM = pl.BlockSpec(memory_space=pltpu.VMEM)
HBM = pl.BlockSpec(memory_space=pltpu.HBM)


def rolled(value, shift, axis):
    shift = shift % value.shape[axis]
    return pltpu.roll(value, shift, axis) if shift else value


def rows_out(main, first):
    split = main.reshape(3, 4, ROWS, C)
    group = lax.broadcasted_iota(jnp.int32, (3, ROWS, C), 1) // 2
    out = None
    for q in range(4):
        piece = rolled(split[:, q], 2 * q - first, 1)
        out = piece if out is None else jnp.where(group == q, piece, out)
    return out.reshape(EDGE, C)


def spread(edge, which, to):
    split = edge.reshape(3, ROWS, C)
    pieces = [rolled(split, to - (2 * q + which), 1) for q in range(4)]
    return jnp.stack(pieces, axis=1).reshape(COLS, ROWS, C)


def shifted_row(main, b, before, before_which, after, after_which):
    if b == 1:
        return main
    split = main.reshape(COLS, ROWS, C)
    place = lax.broadcasted_iota(jnp.int32, (COLS, ROWS, C), 1)
    if b == 0:
        moved = jnp.where(place == 0, spread(before, before_which, 0), rolled(split, 1, 1))
    else:
        moved = jnp.where(place == ROWS - 1, spread(after, after_which, ROWS - 1), rolled(split, -1, 1))
    return moved.reshape(MAIN, C)


def column_taps(main):
    zeros = jnp.zeros((ROWS, C), F32)
    return [
        jnp.concatenate([zeros, main[: MAIN - ROWS]], axis=0),
        main,
        jnp.concatenate([main[ROWS:], zeros], axis=0),
    ]


def edge_column_taps(edge):
    place = lax.broadcasted_iota(jnp.int32, (EDGE, C), 0)
    return [
        jnp.where(place < 2, 0.0, rolled(edge, 2, 0)),
        edge,
        jnp.where(place >= EDGE - 2, 0.0, rolled(edge, -2, 0)),
    ]


def edge_pair(top, bottom):
    even = lax.broadcasted_iota(jnp.int32, (EDGE, C), 0) % 2 == 0
    return jnp.where(even, rolled(top, -1, 0), rolled(bottom, 1, 0))


def normed(values, gain):
    factor = lax.rsqrt(jnp.mean(values * values, axis=-1, keepdims=True) + EPSILON)
    v = values * factor * gain
    return v / (1.0 + jnp.exp(-v))


def push_weights(weights, a, step, slot):
    at = step * TILE
    depth = min(TILE, K - at)
    left = weights[a, at : at + depth, 0:TILE]
    right = weights[a, at : at + depth, TILE:C]
    right = jnp.concatenate([right, right], axis=1)
    if depth < TILE:
        empty = jnp.zeros((TILE - depth, TILE), BF16)
        left = jnp.concatenate([left, empty], axis=0)
        right = jnp.concatenate([right, empty], axis=0)
    pltpu.matmul_push_rhs(left, slot, 0)
    pltpu.matmul_push_rhs(right, slot, 1)


def multiply(accumulators, operand, index, step, slot):
    at = step * TILE
    depth = min(TILE, K - at)
    rows = operand[index][:, at : at + depth] if isinstance(operand, list) else operand[index, :, at : at + depth]
    if depth < TILE:
        rows = jnp.concatenate([rows, rows], axis=1)
    for accumulator in accumulators:
        pltpu.matmul_acc_lhs(accumulator, rows, load_staged_rhs=slot)


def popped(accumulators):
    return jnp.concatenate([pltpu.matmul_pop(accumulators[0]), pltpu.matmul_pop(accumulators[1])[:, : C - TILE]], axis=1)


def woven(steps, thunks):
    order, done = [], 0
    for i, step in enumerate(steps):
        order.append(step)
        due = (i + 1) * len(thunks) // len(steps)
        order += thunks[done:due]
        done = due
    return order


def first_normed(frame, keep, gain):
    return normed(jnp.where(keep, frame.astype(F32), 0.0), gain).astype(BF16)


class Section:
    def __init__(self, refs, accumulators, live, even, at_top, at_bottom):
        self.__dict__.update(refs)
        self.live, self.even, self.at_top, self.at_bottom = live, even, at_top, at_bottom
        frames = FRAMES
        self.sums1 = [(accumulators[f], accumulators[frames + f]) for f in range(frames)]
        self.sums2 = [(accumulators[2 * frames + f], accumulators[3 * frames + f]) for f in range(frames)]
        at = 4 * frames
        self.edges1 = [(accumulators[at + i], accumulators[at + 2 + i]) for i in range(2)]

    def halo(self, f):
        near, far = self.near[f].astype(F32), self.far[f].astype(F32)
        top = jnp.where(self.at_top, 0.0, jnp.where(self.even, far, near))
        bottom = jnp.where(self.at_bottom, 0.0, jnp.where(self.even, near, far))
        return top, bottom

    def norm_first(self, f):
        self.window1[f + 2] = first_normed(self.x[f], f < self.live, self.gain1[...])

    def norm_first_halo(self, f):
        keep = f < self.live
        gain = self.gain1[...]
        top, bottom = (jnp.where(keep, rows, 0.0) for rows in self.halo(f))
        values = jnp.concatenate([top, bottom], axis=0)
        self.halos[f + 2] = normed(values, gain).astype(BF16)

    def build_first_edges(self, g):
        main = self.window1[g].astype(F32)
        halo = self.halos[g].astype(F32)
        top, bottom = halo[:EDGE], halo[EDGE:]
        even = lax.broadcasted_iota(jnp.int32, (EDGE, C), 0) % 2 == 0
        self.edge_rows[g, 0] = jnp.where(even, top, rows_out(main, 6))
        self.edge_rows[g, 1] = edge_pair(top, bottom)
        self.edge_rows[g, 2] = jnp.where(even, rows_out(main, 0), bottom)

    def build_first_pair(self, g, b):
        taps = [edge_column_taps(self.edge_rows[g + i, b]) for i in range(2)]
        for c in range(3):
            at = (3 * b + c) * C
            rows = jnp.concatenate([taps[0][c], taps[1][c]], axis=0)
            self.edges[g, :, at : at + C] = rows.astype(BF16)

    def build_first(self, g, b):
        main = self.window1[g].astype(F32)
        halo = self.halos[g].astype(F32)
        self.build(self.operand1, g, b, main, halo[:EDGE], 1, halo[EDGE:], 0)

    def build_second(self, g, b):
        main = self.window2[g].astype(F32)
        edge = self.hidden_edges[g]
        self.build(self.operand2, g, b, main, edge, 0, edge, 1)

    def build(self, operand, g, b, main, before, before_which, after, after_which):
        rows = shifted_row(main, b, before, before_which, after, after_which)
        for c, taps in enumerate(column_taps(rows)):
            at = (3 * b + c) * C
            operand[g, :, at : at + C] = taps.astype(BF16)

    def first_thunks(self, pair, cached=False):
        out = []
        for g in (pair, pair + 1):
            if not cached:
                out += [lambda f=g - 2: self.norm_first(f)] if self.norms else []
                out += [lambda f=g - 2: self.norm_first_halo(f)]
        for g in (pair, pair + 1):
            out += [lambda g=g: self.build_first_edges(g)]
            out += [lambda g=g, b=b: self.build_first(g, b) for b in range(3)]
        starts = [pair] if pair == 0 else [pair - 1, pair]
        out += [lambda g=g, b=b: self.build_first_pair(g, b) for g in starts for b in range(3)]
        return out

    def second_thunks(self, pair, cached=False):
        out = []
        if not cached:
            out += [lambda f=f: self.norm_second(f) for f in (pair - 2, pair - 1)]
            out += [lambda i=pair // 2 - 1: self.norm_second_edges(i)]
        out += [lambda g=g, b=b: self.build_second(g, b) for g in (pair, pair + 1) for b in range(3)]
        return out

    def norm_second(self, f):
        hidden = popped(self.sums1[f]) + self.bias1[...]
        if self.early1 is not None and f < 2:
            hidden = hidden + self.early1[f]
        hidden = jnp.where(f < self.live, hidden, 0.0)
        self.window2[f + 2] = normed(hidden, self.gain2[...]).astype(BF16)

    def norm_second_edges(self, i):
        hidden = popped(self.edges1[i]) + self.bias1[...]
        if self.early1 is not None and i == 0:
            hidden = hidden + self.early_edges[...]
        place = lax.broadcasted_iota(jnp.int32, (2 * EDGE, C), 0)
        outside = ((place % 2 == 0) & self.at_top) | ((place % 2 == 1) & self.at_bottom)
        hidden = jnp.where(outside, 0.0, hidden)
        values = normed(hidden, self.gain2[...]).astype(BF16).astype(F32)
        for j in range(2):
            f = 2 * i + j
            self.hidden_edges[f + 2] = jnp.where(f < self.live, values[j * EDGE : (j + 1) * EDGE], 0.0)

    def final(self, f):
        result = popped(self.sums2[f]) + self.bias2[...] + self.x[f].astype(F32)
        if self.early1 is not None and f < 2:
            result = result + self.early2[f]
        return jnp.where(f < self.live, result, 0.0).astype(BF16)

    def phase(self, conv, pair):
        weights = (self.weights1, self.weights2)[conv]
        operand = (self.operand1, self.operand2)[conv]
        sums = (self.sums1, self.sums2)[conv]
        steps = []
        for a in range(3):
            work = [(sums[g - a], operand, g) for g in (pair, pair + 1) if 0 <= g - a < FRAMES]
            if conv == 0:
                for i in range(2):
                    if pair <= 2 * i + a + 1 < pair + 2:
                        work.append((self.edges1[i], self.edges, 2 * i + a))
            if work:
                steps += [(conv, a, step, weights, work) for step in range(STEPS)]
        return steps

    def run(self, order):
        steps = [entry for entry in order if isinstance(entry, tuple)]

        def push(i):
            _, a, step, weights, _ = steps[i]
            push_weights(weights, a, step, i % 2)

        i = 0
        for entry in order:
            if not isinstance(entry, tuple):
                entry()
                continue
            if i == 0:
                push(0)
            if i + 1 < len(steps):
                push(i + 1)
            _, _, step, _, work = entry
            for n, (accumulators, operand, g) in enumerate(work):
                multiply(accumulators, operand, g, step, i % 2 if n == 0 else None)
            i += 1


def edges_out(main, even, near, far, f):
    upper, lower = rows_out(main, 0), rows_out(main, 6)
    near[f] = jnp.where(even, lower, upper).astype(BF16)
    far[f] = jnp.where(even, upper, lower).astype(BF16)


def pack_kernel(x, first, second, near, far):
    even = lax.axis_index("strip") % 2 == 0
    for source, start in ((x, 0), (first, 4), (second, 6)):
        for f in range(source.shape[0]):
            edges_out(source[f].astype(F32), even, near, far, start + f)


WINDOW = (FRAMES + 2, MAIN, C)
OPERANDS = dict(
    edge_rows=pltpu.VMEM((FRAMES + 2, 3, EDGE, C), F32),
    operand1=pltpu.VMEM((FRAMES + 2, MAIN, K), BF16),
    edges=pltpu.VMEM((FRAMES + 1, 2 * EDGE, K), BF16),
    operand2=pltpu.VMEM((FRAMES + 2, MAIN, K), BF16),
)
VECTORS = ("bias1", "gain1", "bias2", "gain2")


def live_frames(counts, tick):
    return counts[7 - lax.axis_index("segment") + tick]


def with_section(given, live, body):
    strip = lax.axis_index("strip")
    given = {"early1": None, **given}

    def inner(*accumulators):
        body(Section(given, accumulators, live, strip % 2 == 0, strip == 0, strip == lax.axis_size("strip") - 1))

    shapes = [MAIN] * (4 * FRAMES) + [2 * EDGE] * 4
    units = ([0] * FRAMES + [1] * FRAMES) * 2 + [0, 0, 1, 1]
    pl.run_scoped(inner, *[pltpu.ACC(unit)((rows, TILE), F32) for unit, rows in zip(units, shapes)])


def prepare_kernel(r):
    pairs = [(r[n + "_hbm"], r[n]) for n in ("x", "gain1", "bias1", "gain2", "bias2", "second", "incoming")]
    pairs += [(r["counts_hbm"], r["counts"]), (r["first_hbm"], r["window1"].at[pl.ds(0, 2)])]
    pairs += [(r["weights1_hbm"].at[a], r["weights1"].at[a]) for a in range(3)]
    copies = [pltpu.make_async_copy(source, target, r["sems"].at[i]) for i, (source, target) in enumerate(pairs)]
    for copy in copies:
        copy.start()
    copies[7].wait()
    copies[0].wait()
    copies[1].wait()
    live = live_frames(r["counts"], 0)
    gain = r["gain1"][...]
    for f in range(FRAMES):
        r["window1"][f + 2] = first_normed(r["x"][f], f < live, gain)
    for i, copy in enumerate(copies):
        if i not in (0, 1, 7):
            copy.wait()


def tick0_kernel(r):
    counting = pltpu.make_async_copy(r["counts_hbm"], r["counts"], r["sems"].at[3])
    counting.start()
    copies = [pltpu.make_async_copy(r["weights2_hbm"].at[a], r["weights2"].at[a], r["sems"].at[a]) for a in range(3)]
    for copy in copies:
        copy.start()
    counting.wait()
    live = live_frames(r["counts"], 0)

    def body(work):
        work.norms = False
        work.window2[0:2] = work.second[...]
        for g in range(2):
            work.halos[g] = jnp.concatenate(work.halo(4 + g), axis=0).astype(BF16)
            work.hidden_edges[g] = edge_pair(*work.halo(6 + g))
        order = work.first_thunks(0, cached=True)
        order += woven(work.phase(0, 0), work.first_thunks(2))
        order += woven(work.phase(0, 2), work.first_thunks(4) + work.second_thunks(0, cached=True))
        order += woven(work.phase(0, 4), work.second_thunks(2))
        at = max(i for i, entry in enumerate(order) if isinstance(entry, tuple))
        order[at:at] = [copy.wait for copy in copies]
        order += woven(work.phase(1, 0), work.second_thunks(4))
        order += work.phase(1, 2) + work.phase(1, 4)
        work.run(order)
        last = lax.axis_index("segment") == lax.axis_size("segment") - 1
        for f in range(FRAMES):
            result = work.final(f)
            work.result[f] = result
            passed = jnp.where(last, work.incoming[f].astype(F32), result.astype(F32))
            work.send[f] = passed.astype(BF16)
            edges_out(passed, work.even, work.send_near, work.send_far, f)

    with_section(r, live, body)


def between_kernel(r):
    writing = pltpu.make_async_copy(r["result"], r["whole"].at[0], r["sems"].at[0])
    writing.start()
    counting = pltpu.make_async_copy(r["counts_hbm"], r["counts"], r["sems"].at[1])
    counting.start()
    counting.wait()
    live = live_frames(r["counts"], 0)
    for i in range(2):
        r["first"][i] = r["window1_old"][live + i]
        r["first_halo"][i] = r["halos_old"][live + i]
        r["second"][i] = r["window2_old"][live + i]
        r["second_edge"][i] = r["edges_old"][live + i]

    def body(work):
        order = work.first_thunks(0, cached=True)
        order += woven(work.phase(0, 0), work.second_thunks(0, cached=True))
        order += work.phase(1, 0)
        work.run(order)
        for f in range(2):
            work.sum1[f] = popped(work.sums1[f])
            work.sum2[f] = popped(work.sums2[f])
        work.sum_edges[...] = popped(work.edges1[0])

    given = dict(r, window1=r["first"], halos=r["first_halo"], window2=r["second"], hidden_edges=r["second_edge"])
    with_section(given, live, body)
    writing.wait()


def tick1_kernel(r):
    counting = pltpu.make_async_copy(r["counts_hbm"], r["counts"], r["sems"].at[0])
    counting.start()
    counting.wait()
    live = live_frames(r["counts"], 1)
    copies = []

    def send(source, target):
        copies.append(pltpu.make_async_copy(source, target, r["sems"].at[len(copies) + 1]))
        copies[-1].start()

    def body(work):
        work.norms = True
        for i in range(2):
            work.window1[i] = work.first[i]
            work.halos[i] = work.first_halo[i]
            work.window2[i] = work.second[i]
            work.hidden_edges[i] = work.second_edge[i]
        order = [lambda: work.build_first_edges(1)] + work.first_thunks(2)
        order += woven(work.phase(0, 2), work.first_thunks(4))
        order += [lambda: send(work.window1.at[pl.ds(live, 2)], work.first_next)]
        order += woven(work.phase(0, 4), work.second_thunks(2))
        order += woven(work.phase(1, 2), work.second_thunks(4))
        order += [lambda: send(work.window2.at[pl.ds(live, 2)], work.second_next)]
        order += work.phase(1, 4)
        work.run(order)
        for f in range(FRAMES):
            work.result[f] = work.final(f)
            send(work.result.at[f], work.whole.at[1, f])
        for copy in copies:
            copy.wait()

    with_section(r, live, body)


def call(kernel, operands, outputs, scratch, flops=0, moved=0):
    inputs = list(operands)
    names = inputs + list(outputs) + list(scratch)
    in_hbm = [n.endswith("_hbm") or n == "base" for n in inputs]
    values = [
        pltpu.with_memory_space_constraint(v, pltpu.HBM) if n.endswith("_hbm") else v for n, v in operands.items()
    ]
    aliases = {inputs.index("base"): list(outputs).index("whole")} if "base" in inputs else {}
    results = pl.pallas_call(
        lambda *refs: kernel(dict(zip(names, refs))),
        out_shape=list(outputs.values()),
        in_specs=[HBM if there else VMEM for there in in_hbm],
        out_specs=[HBM if n in ("whole", "first_next", "second_next") else VMEM for n in outputs],
        input_output_aliases=aliases,
        scratch_shapes=list(scratch.values()),
        compiler_params=pltpu.CompilerParams(vmem_limit_bytes=22 << 20),
        cost_estimate=pl.CostEstimate(flops=flops, bytes_accessed=moved, transcendentals=0),
        name=kernel.__name__.removesuffix("_kernel"),
    )(*values)
    return dict(zip(outputs, results))


def shape(*dims):
    return jax.ShapeDtypeStruct(dims, BF16)


def flat(array):
    frames = array.shape[0]
    return array.transpose(0, 2, 1, 3).reshape(frames, MAIN, C)


def unflat(array):
    frames = array.shape[0]
    return array.reshape(frames, COLS, ROWS, C).transpose(0, 2, 1, 3)


def on_device(
    held_blocks,
    incoming,
    frame_counts,
    first_cache,
    second_cache,
    first_kernel,
    first_bias,
    first_gain,
    second_kernel,
    second_bias,
    second_gain,
):
    segments = lax.axis_size("segment")
    strips = lax.axis_size("strip")
    swaps = [
        [(i, i ^ 1) for i in range(strips)],
        [(i, i if i in (0, strips - 1) else ((i + 1) ^ 1) - 1) for i in range(strips)],
    ]
    x = flat(held_blocks[0])
    first = flat(first_cache[0])
    second = flat(second_cache[0])
    near, far = pl.pallas_call(
        pack_kernel,
        out_shape=[pltpu.VMEM((8, EDGE, C), BF16)] * 2,
        in_specs=[VMEM] * 3,
        out_specs=[VMEM] * 2,
        compiler_params=pltpu.CompilerParams(vmem_limit_bytes=8 << 20),
        name="pack",
    )(*(pltpu.with_memory_space_constraint(rows, pltpu.HBM) for rows in (x, first, second)))
    near, far = (lax.ppermute(rows, "strip", swap) for rows, swap in zip((near, far), swaps))
    counts = dict(counts_hbm=frame_counts)
    count_scratch = dict(counts=pltpu.SMEM((9,), jnp.int32), sems=pltpu.SemaphoreType.DMA((16,)))
    block = pltpu.VMEM((FRAMES, MAIN, C), BF16)
    cached = pltpu.VMEM((2, MAIN, C), BF16)
    weights = pltpu.VMEM((3, K, C), BF16)
    ready = call(
        prepare_kernel,
        dict(
            x_hbm=x,
            first_hbm=first,
            second_hbm=second,
            incoming_hbm=flat(incoming[0]),
            bias1_hbm=first_bias,
            gain1_hbm=first_gain,
            bias2_hbm=second_bias,
            gain2_hbm=second_gain,
            weights1_hbm=first_kernel[0].reshape(3, K, C),
            **counts,
        ),
        dict(
            x=block,
            second=cached,
            incoming=block,
            window1=pltpu.VMEM(WINDOW, BF16),
            weights1=weights,
            **{n: pltpu.VMEM((1, C), F32) for n in VECTORS},
        ),
        count_scratch,
        moved=2 * 3 * K * C,
    )
    vectors = {n: ready[n] for n in VECTORS}
    done = call(
        tick0_kernel,
        dict(**counts, near=near, far=far, weights2_hbm=second_kernel[0].reshape(3, K, C), **ready),
        dict(
            weights2=weights,
            halos=pltpu.VMEM((FRAMES + 2, 2 * EDGE, C), BF16),
            window2=pltpu.VMEM(WINDOW, BF16),
            hidden_edges=pltpu.VMEM((FRAMES + 2, EDGE, C), F32),
            result=block,
            send=shape(FRAMES, MAIN, C),
            send_near=shape(FRAMES, EDGE, C),
            send_far=shape(FRAMES, EDGE, C),
        ),
        {**OPERANDS, **count_scratch},
    )

    def onward(rows, swap):
        pairs = [(s * strips + i, (s + 1) % segments * strips + j) for s in range(segments) for i, j in swap]
        return lax.ppermute(rows, ("segment", "strip"), pairs)

    x = onward(done["send"], [(i, i) for i in range(strips)])
    near, far = (onward(done[n], swap) for n, swap in zip(("send_near", "send_far"), swaps))
    both = dict(weights1=ready["weights1"], weights2=done["weights2"])
    early = call(
        between_kernel,
        dict(
            **counts,
            window1_old=ready["window1"],
            halos_old=done["halos"],
            window2_old=done["window2"],
            edges_old=done["hidden_edges"],
            result=done["result"],
            **both,
        ),
        dict(
            whole=shape(2, FRAMES, MAIN, C),
            first=cached,
            first_halo=pltpu.VMEM((2, 2 * EDGE, C), BF16),
            second=cached,
            second_edge=pltpu.VMEM((2, EDGE, C), F32),
            sum1=pltpu.VMEM((2, MAIN, C), F32),
            sum_edges=pltpu.VMEM((2 * EDGE, C), F32),
            sum2=pltpu.VMEM((2, MAIN, C), F32),
        ),
        {**OPERANDS, **count_scratch},
        flops=2 * 2 * 3 * MAIN * K * C,
        moved=2 * 3 * K * C,
    )
    whole = early.pop("whole")
    for name, sums in (("early1", "sum1"), ("early_edges", "sum_edges"), ("early2", "sum2")):
        early[name] = early.pop(sums)
    out = call(
        tick1_kernel,
        dict(**counts, x=x, near=near, far=far, **early, **both, **vectors, base=whole),
        dict(whole=shape(2, FRAMES, MAIN, C), first_next=shape(2, MAIN, C), second_next=shape(2, MAIN, C)),
        dict(
            window1=pltpu.VMEM(WINDOW, BF16),
            halos=pltpu.VMEM((FRAMES + 2, 2 * EDGE, C), BF16),
            window2=pltpu.VMEM(WINDOW, BF16),
            hidden_edges=pltpu.VMEM((FRAMES + 2, EDGE, C), F32),
            result=block,
            **OPERANDS,
            **count_scratch,
        ),
    )
    return (
        unflat(out["whole"].reshape(2 * FRAMES, MAIN, C)).reshape(2, 1, FRAMES, ROWS, COLS, C),
        unflat(out["first_next"])[None],
        unflat(out["second_next"])[None],
    )


def solution(mesh):
    return jax.shard_map(
        on_device,
        mesh=mesh,
        in_specs=(
            P("segment", None, "strip", None, None),
            P(None, None, "strip", None, None),
            P(),
            P("segment", None, "strip", None, None),
            P("segment", None, "strip", None, None),
            P("segment", None, None, None, None, None),
            P("segment", None),
            P("segment", None),
            P("segment", None, None, None, None, None),
            P("segment", None),
            P("segment", None),
        ),
        out_specs=(
            P(None, "segment", None, "strip", None, None),
            P("segment", None, "strip", None, None),
            P("segment", None, "strip", None, None),
        ),
        check_vma=False,
    )
```

```python
import jax
import jax.numpy as jnp
from jax import lax
from jax.experimental import pallas as pl
from jax.experimental.pallas import tpu as pltpu
from jax.sharding import PartitionSpec as P

EPSILON = 1e-06
C = 384
FRAMES = 4
COLS = 12
ROWS = 8
MAIN = COLS * ROWS
EDGE = COLS * 2
TAPS = 9
K = TAPS * C
TILE = 256
STEPS = -(-K // TILE)
BF16 = jnp.bfloat16
F32 = jnp.float32
VMEM = pl.BlockSpec(memory_space=pltpu.VMEM)
HBM = pl.BlockSpec(memory_space=pltpu.HBM)


def rolled(value, shift, axis):
    shift = shift % value.shape[axis]
    return pltpu.roll(value, shift, axis) if shift else value


def rows_out(main, first):
    split = main.reshape(3, 4, ROWS, C)
    group = lax.broadcasted_iota(jnp.int32, (3, ROWS, C), 1) // 2
    out = None
    for q in range(4):
        piece = rolled(split[:, q], 2 * q - first, 1)
        out = piece if out is None else jnp.where(group == q, piece, out)
    return out.reshape(EDGE, C)


def spread(edge, which, to):
    split = edge.reshape(3, ROWS, C)
    pieces = [rolled(split, to - (2 * q + which), 1) for q in range(4)]
    return jnp.stack(pieces, axis=1).reshape(COLS, ROWS, C)


def shifted_row(main, b, before, before_which, after, after_which):
    if b == 1:
        return main
    split = main.reshape(COLS, ROWS, C)
    place = lax.broadcasted_iota(jnp.int32, (COLS, ROWS, C), 1)
    if b == 0:
        moved = jnp.where(place == 0, spread(before, before_which, 0), rolled(split, 1, 1))
    else:
        moved = jnp.where(place == ROWS - 1, spread(after, after_which, ROWS - 1), rolled(split, -1, 1))
    return moved.reshape(MAIN, C)


def column_taps(main):
    zeros = jnp.zeros((ROWS, C), F32)
    return [
        jnp.concatenate([zeros, main[: MAIN - ROWS]], axis=0),
        main,
        jnp.concatenate([main[ROWS:], zeros], axis=0),
    ]


def edge_column_taps(edge):
    place = lax.broadcasted_iota(jnp.int32, (EDGE, C), 0)
    return [
        jnp.where(place < 2, 0.0, rolled(edge, 2, 0)),
        edge,
        jnp.where(place >= EDGE - 2, 0.0, rolled(edge, -2, 0)),
    ]


def edge_pair(top, bottom):
    even = lax.broadcasted_iota(jnp.int32, (EDGE, C), 0) % 2 == 0
    return jnp.where(even, rolled(top, -1, 0), rolled(bottom, 1, 0))


def normed(values, gain):
    factor = lax.rsqrt(jnp.mean(values * values, axis=-1, keepdims=True) + EPSILON)
    v = values * factor * gain
    return v / (1.0 + jnp.exp(-v))


def weight_tile(weights, taps, step):
    at = step * TILE
    depth = min(TILE, K - at)
    if len(taps) == 1:
        tile = weights[taps[0], at : at + depth, 0:TILE]
    else:
        empty = jnp.zeros((depth, C - TILE), BF16)
        tile = jnp.concatenate(
            [empty if a is None else weights[a, at : at + depth, TILE:C] for a in taps], axis=1
        )
    if depth < TILE:
        tile = jnp.concatenate([tile, jnp.zeros((TILE - depth, TILE), BF16)], axis=0)
    return tile


def multiply(accumulator, operand, index, step, slot):
    at = step * TILE
    depth = min(TILE, K - at)
    rows = operand[index, :, at : at + depth]
    if depth < TILE:
        rows = jnp.concatenate([rows, rows], axis=1)
    pltpu.matmul_acc_lhs(accumulator, rows, load_staged_rhs=slot)


def halves(accumulator):
    both = pltpu.matmul_pop(accumulator)
    return both[:, : C - TILE], both[:, C - TILE :]


def timeline(phases, groups):
    clock, starts, ends, entries = [0, 0], {}, {}, []
    for name, units in phases:
        for unit, steps in enumerate(units):
            starts[name, unit] = clock[unit]
            for step in steps:
                entries.append((clock[unit], 1, len(entries), step))
                clock[unit] += sum(operand.shape[1] for _, operand, _ in step[4])
            ends[name, unit] = clock[unit]
    for after, before, thunks in groups:
        first = max(ends[after, 0], ends[after, 1]) if after else -1
        last = min(starts[before, 0], starts[before, 1]) if before else max(clock) + 1
        last = max(last, first + 1)
        for i, thunk in enumerate(thunks):
            entries.append((first + (last - first) * i / len(thunks), 0, len(entries), thunk))
    return [entry[3] for entry in sorted(entries, key=lambda entry: entry[:3])]


def first_normed(frame, keep, gain):
    return normed(jnp.where(keep, frame.astype(F32), 0.0), gain).astype(BF16)


class Section:
    def __init__(self, refs, accumulators, even, at_top, at_bottom):
        self.__dict__.update(refs)
        self.even, self.at_top, self.at_bottom = even, at_top, at_bottom
        at = 0
        for name, (_, _, count) in ACCUMULATORS.items():
            setattr(self, name, accumulators[at : at + count])
            at += count
        self.left = [self.left[:4], self.left[:2] + self.left[4:]]
        self.right = [self.right[:5], self.right[:3] + self.right[5:] + self.right[4:5]]
        self.saved = None

    def halo(self, f):
        near, far = self.near[f].astype(F32), self.far[f].astype(F32)
        top = jnp.where(self.at_top, 0.0, jnp.where(self.even, far, near))
        bottom = jnp.where(self.at_bottom, 0.0, jnp.where(self.even, near, far))
        return top, bottom

    def norm_first(self, f):
        self.window1[f + 2] = normed(self.x[f].astype(F32), self.gain1[...]).astype(BF16)

    def norm_first_halo(self, f):
        gain = self.gain1[...]
        values = jnp.concatenate(self.halo(f), axis=0)
        self.halos[f + 2] = normed(values, gain).astype(BF16)

    def build_first_edges(self, g):
        main = self.window1[g].astype(F32)
        halo = self.halos[g].astype(F32)
        top, bottom = halo[:EDGE], halo[EDGE:]
        even = lax.broadcasted_iota(jnp.int32, (EDGE, C), 0) % 2 == 0
        self.edge_rows[g, 0] = jnp.where(even, top, rows_out(main, 6))
        self.edge_rows[g, 1] = edge_pair(top, bottom)
        self.edge_rows[g, 2] = jnp.where(even, rows_out(main, 0), bottom)

    def build_first_pair(self, g, b):
        taps = [edge_column_taps(self.edge_rows[g + i, b]) for i in range(2)]
        for c in range(3):
            at = (3 * b + c) * C
            rows = jnp.concatenate([taps[0][c], taps[1][c]], axis=0)
            self.edges[g, :, at : at + C] = rows.astype(BF16)

    def build_first(self, g, b):
        main = self.window1[g].astype(F32)
        halo = self.halos[g].astype(F32)
        self.build(self.operand1, g, b, main, halo[:EDGE], 1, halo[EDGE:], 0)

    def build_second(self, g, b):
        main = self.window2[g].astype(F32)
        edge = self.hidden_edges[g]
        self.build(self.operand2, g, b, main, edge, 0, edge, 1)

    def build(self, operand, g, b, main, before, before_which, after, after_which):
        rows = shifted_row(main, b, before, before_which, after, after_which)
        for c, taps in enumerate(column_taps(rows)):
            at = (3 * b + c) * C
            operand[g, :, at : at + C] = taps.astype(BF16)

    def first_thunks(self, pair, cached=False):
        out = []
        for g in (pair, pair + 1):
            if not cached:
                out += [lambda f=g - 2: self.norm_first(f)] if self.norms else []
                out += [lambda f=g - 2: self.norm_first_halo(f)]
        for g in (pair, pair + 1):
            out += [lambda g=g: self.build_first_edges(g)]
            out += [lambda g=g, b=b: self.build_first(g, b) for b in range(3)]
        starts = [pair] if pair == 0 else [pair - 1, pair]
        out += [lambda g=g, b=b: self.build_first_pair(g, b) for g in starts for b in range(3)]
        return out

    def second_thunks(self, pair, cached=False):
        out = []
        if not cached:
            out += [lambda f=f: self.norm_second(f) for f in (pair - 2, pair - 1)]
            out += [lambda i=pair // 2 - 1: self.norm_second_edges(i)]
        out += [lambda g=g, b=b: self.build_second(g, b) for g in (pair, pair + 1) for b in range(3)]
        return out

    def pop_sums(self, conv, f):
        left = pltpu.matmul_pop(self.left[conv][f])
        if f < 2 and conv in self.moved:
            left = left + pltpu.matmul_pop(self.moved_left[f])
        if f == 0:
            self.saved = halves(self.right[conv][0])[0] if self.early1 is None else 0.0
        right, (following, second) = self.saved, halves(self.right[conv][f + 1])
        self.saved = following
        sums = jnp.concatenate([left, right + second], axis=1)
        if self.early1 is not None and f < 2:
            sums = sums + (self.early1, self.early2)[conv][f]
        return sums

    def pop_edges(self, i):
        left = pltpu.matmul_pop(self.left_edges[i])
        if i == 0 and 0 in self.moved:
            left = left + pltpu.matmul_pop(self.moved_edges[0])
        if i or self.early1 is None:
            right = halves(self.right_edges[i])[0] + halves(self.right_edges[2 + i])[1]
        else:
            right = halves(self.right_edges[2])[1]
        sums = jnp.concatenate([left, right], axis=1)
        return sums + self.early_edges[...] if self.early1 is not None and i == 0 else sums

    def norm_second(self, f):
        hidden = jnp.where(f < self.live(), self.pop_sums(0, f) + self.bias1[...], 0.0)
        self.window2[f + 2] = normed(hidden, self.gain2[...]).astype(BF16)

    def norm_second_edges(self, i):
        hidden = self.pop_edges(i) + self.bias1[...]
        place = lax.broadcasted_iota(jnp.int32, (2 * EDGE, C), 0)
        outside = ((place % 2 == 0) & self.at_top) | ((place % 2 == 1) & self.at_bottom)
        hidden = jnp.where(outside, 0.0, hidden)
        values = normed(hidden, self.gain2[...]).astype(BF16).astype(F32)
        for j in range(2):
            f = 2 * i + j
            self.hidden_edges[f + 2] = jnp.where(f < self.live(), values[j * EDGE : (j + 1) * EDGE], 0.0)

    def final(self, f):
        result = self.pop_sums(1, f) + self.bias2[...] + self.x[f].astype(F32)
        return jnp.where(f < self.live(), result, 0.0).astype(BF16)

    def phase(self, conv, pair):
        weights = (self.weights1, self.weights2)[conv]
        operand = (self.operand1, self.operand2)[conv]
        moved = conv in self.moved
        units = ([], [])

        def add(unit, taps, work, edge_work=()):
            work = [(accumulator, operand, g) for accumulator, g in work]
            if conv == 0:
                work += [(accumulator, self.edges, g) for accumulator, g in edge_work]
            units[unit].extend((unit, taps, step, weights, work) for step in range(STEPS))

        left, right = self.left[conv], self.right[conv]
        for a in range(3):
            work = [(left[g - a], g) for g in (pair, pair + 1) if 0 <= g - a < FRAMES]
            edge_work = [(self.left_edges[i], 2 * i + a) for i in range(2) if pair <= 2 * i + a + 1 < pair + 2]
            if moved and pair == 2 and a == 2:
                work = [(self.moved_left[f], f + 2) for f in range(2)]
                add(1, (2,), work, [(self.moved_edges[0], 2)])
            elif work:
                add(0, (a,), work, edge_work)
        edges = self.right_edges
        if pair == 0:
            add(1, (0, 1), [(right[0], 0), (right[1], 1)], [(edges[0], 0)])
        elif pair == 2:
            add(1, (0, 1), [(right[2], 2), (right[3], 3)], [(edges[2], 1), (edges[1], 2)])
            add(1, (None, 2), [(right[1], 2), (right[2], 3)], [(edges[2], 2)])
        else:
            add(1, (1, 2), [(right[3], 4), (right[4], 5)], [(edges[1], 3), (edges[3], 4)])
        return (conv, pair), units

    def run(self, order):
        steps = [[entry for entry in order if isinstance(entry, tuple) and entry[0] == unit] for unit in range(2)]
        count = [0, 0]

        def push(unit, i):
            _, taps, step, weights, _ = steps[unit][i]
            pltpu.matmul_push_rhs(weight_tile(weights, taps, step), i % 2, unit)

        for entry in order:
            if not isinstance(entry, tuple):
                entry()
                continue
            unit, _, step, _, work = entry
            i = count[unit]
            count[unit] += 1
            if i == 0:
                push(unit, 0)
            if i + 1 < len(steps[unit]):
                push(unit, i + 1)
            for n, (accumulator, operand, g) in enumerate(work):
                multiply(accumulator, operand, g, step, i % 2 if n == 0 else None)


def edges_out(main, even, near, far, f):
    upper, lower = rows_out(main, 0), rows_out(main, 6)
    near[f] = jnp.where(even, lower, upper).astype(BF16)
    far[f] = jnp.where(even, upper, lower).astype(BF16)


def pack_kernel(counts_hbm, x, first, second, near, far, counts, sem):
    counting = pltpu.make_async_copy(counts_hbm, counts, sem)
    counting.start()
    even = lax.axis_index("strip") % 2 == 0
    for source, start in ((first, 4), (second, 6), (x, 0)):
        if start == 0:
            counting.wait()
        for f in range(source.shape[0]):
            rows = source[f].astype(F32)
            if start == 0:
                rows = jnp.where(f < live_frames(counts, 0), rows, 0.0)
            edges_out(rows, even, near, far, start + f)


WINDOW = (FRAMES + 2, MAIN, C)
OPERANDS = dict(
    edge_rows=pltpu.VMEM((FRAMES + 2, 3, EDGE, C), F32),
    operand1=pltpu.VMEM((FRAMES + 2, MAIN, K), BF16),
    edges=pltpu.VMEM((FRAMES + 1, 2 * EDGE, K), BF16),
    operand2=pltpu.VMEM((FRAMES + 2, MAIN, K), BF16),
)
VECTORS = ("bias1", "gain1", "bias2", "gain2")


def live_frames(counts, tick):
    return counts[7 - lax.axis_index("segment") + tick]


ACCUMULATORS = dict(
    left=(0, MAIN, FRAMES + 2),
    left_edges=(0, 2 * EDGE, 2),
    right=(1, MAIN, FRAMES + 2),
    right_edges=(1, 2 * EDGE, 4),
    moved_left=(1, MAIN, 2),
    moved_edges=(1, 2 * EDGE, 1),
)


def with_section(given, body):
    strip = lax.axis_index("strip")
    given = {"early1": None, **given}

    def inner(*accumulators):
        body(Section(given, accumulators, strip % 2 == 0, strip == 0, strip == lax.axis_size("strip") - 1))

    shapes = [pltpu.ACC(unit)((rows, TILE), F32) for unit, rows, count in ACCUMULATORS.values() for _ in range(count)]
    pl.run_scoped(inner, *shapes)


def prepare_kernel(r):
    pairs = [(r[n + "_hbm"], r[n]) for n in ("x", "gain1", "bias1", "gain2", "bias2", "second", "incoming")]
    pairs += [(r["counts_hbm"], r["counts"]), (r["first_hbm"], r["window1"].at[pl.ds(0, 2)])]
    pairs += [(r["weights1_hbm"].at[a], r["weights1"].at[a]) for a in range(3)]
    copies = [pltpu.make_async_copy(source, target, r["sems"].at[i]) for i, (source, target) in enumerate(pairs)]
    for copy in copies:
        copy.start()
    copies[7].wait()
    copies[0].wait()
    copies[1].wait()
    live = live_frames(r["counts"], 0)
    gain = r["gain1"][...]
    for f in range(FRAMES):
        r["window1"][f + 2] = first_normed(r["x"][f], f < live, gain)
    for i, copy in enumerate(copies):
        if i not in (0, 1, 7):
            copy.wait()


def tick0_kernel(r):
    counting = pltpu.make_async_copy(r["counts_hbm"], r["counts"], r["sems"].at[3])
    counting.start()
    copies = [pltpu.make_async_copy(r["weights2_hbm"].at[a], r["weights2"].at[a], r["sems"].at[a]) for a in range(3)]
    for copy in copies:
        copy.start()

    def body(work):
        work.norms = False
        work.moved = (0, 1)
        work.live = lambda: live_frames(r["counts"], 0)
        work.window2[0:2] = work.second[...]
        for g in range(2):
            work.halos[g] = jnp.concatenate(work.halo(4 + g), axis=0).astype(BF16)
            work.hidden_edges[g] = edge_pair(*work.halo(6 + g))
        last = lax.axis_index("segment") == lax.axis_size("segment") - 1

        def finish(f):
            result = work.final(f)
            work.result[f] = result
            fresh = jnp.where(f < r["counts"][8], work.incoming[f].astype(F32), 0.0)
            passed = jnp.where(last, fresh, result.astype(F32))
            work.send[f] = passed.astype(BF16)
            edges_out(passed, work.even, work.send_near, work.send_far, f)

        finishing = [lambda f=f: finish(f) for f in range(FRAMES)]
        phases = [work.phase(conv, pair) for conv in range(2) for pair in (0, 2, 4)]
        groups = [
            (None, (0, 0), work.first_thunks(0, cached=True)),
            (None, (0, 2), work.first_thunks(2)),
            ((0, 0), (0, 4), work.first_thunks(4)),
            ((0, 0), (0, 4), work.second_thunks(0, cached=True)),
            ((0, 0), (0, 4), [counting.wait]),
            ((0, 2), (1, 0), [copy.wait for copy in copies]),
            ((0, 2), (1, 0), work.second_thunks(2)),
            ((0, 4), (1, 2), work.second_thunks(4)),
            ((1, 2), None, finishing[:2]),
        ]
        work.run(timeline(phases, groups) + finishing[2:])

    with_section(r, body)


def between_kernel(r):
    writing = pltpu.make_async_copy(r["result"], r["whole"].at[0], r["sems"].at[0])
    writing.start()
    counting = pltpu.make_async_copy(r["counts_hbm"], r["counts"], r["sems"].at[1])
    counting.start()
    counting.wait()
    live = live_frames(r["counts"], 0)
    for i in range(2):
        r["first"][i] = r["window1_old"][live + i]
        r["first_halo"][i] = r["halos_old"][live + i]
        r["second"][i] = r["window2_old"][live + i]
        r["second_edge"][i] = r["edges_old"][live + i]

    def body(work):
        work.moved = ()

        def store(conv, sums):
            for f in range(2):
                right, second = halves(work.right[conv][f])
                if f == 1:
                    sums[0, :, TILE:C] += second
                sums[f, :, 0:TILE] = pltpu.matmul_pop(work.left[conv][f])
                sums[f, :, TILE:C] = right
            if conv == 0:
                work.sum_edges[:, 0:TILE] = pltpu.matmul_pop(work.left_edges[0])
                work.sum_edges[:, TILE:C] = halves(work.right_edges[0])[0]

        order = work.first_thunks(0, cached=True)
        order += timeline([work.phase(0, 0)], [(None, None, work.second_thunks(0, cached=True))])
        order += [lambda: store(0, work.sum1)]
        order += timeline([work.phase(1, 0)], [])
        work.run(order)
        store(1, work.sum2)

    given = dict(r, window1=r["first"], halos=r["first_halo"], window2=r["second"], hidden_edges=r["second_edge"])
    with_section(given, body)
    writing.wait()


def tick1_kernel(r):
    counting = pltpu.make_async_copy(r["counts_hbm"], r["counts"], r["sems"].at[0])
    counting.start()
    copies = []

    def send(source, target):
        copies.append(pltpu.make_async_copy(source, target, r["sems"].at[len(copies) + 1]))
        copies[-1].start()

    def body(work):
        work.norms = True
        work.moved = (1,)
        work.live = lambda: live_frames(r["counts"], 1)
        for i in range(2):
            work.window1[i] = work.first[i]
            work.halos[i] = work.first_halo[i]
            work.window2[i] = work.second[i]
            work.hidden_edges[i] = work.second_edge[i]

        def finish(f):
            work.result[f] = work.final(f)
            send(work.result.at[f], work.whole.at[1, f])

        def send_window(window, target):
            send(window.at[pl.ds(work.live(), 2)], target)

        finishing = [lambda f=f: finish(f) for f in range(FRAMES)]
        phases = [work.phase(conv, pair) for conv in range(2) for pair in (2, 4)]
        groups = [
            (None, (0, 4), work.first_thunks(4)),
            (None, (0, 4), [counting.wait]),
            ((0, 2), (1, 2), work.second_thunks(2)),
            ((0, 2), (1, 2), [lambda: send_window(work.window1, work.first_next)]),
            ((0, 4), (1, 4), work.second_thunks(4)),
            ((1, 2), None, finishing[:2]),
        ]
        order = [lambda: work.build_first_edges(1)] + work.first_thunks(2) + timeline(phases, groups)
        work.run(order + [lambda: send_window(work.window2, work.second_next)] + finishing[2:])
        for copy in copies:
            copy.wait()

    with_section(r, body)


def call(kernel, operands, outputs, scratch, flops=0, moved=0):
    inputs = list(operands)
    names = inputs + list(outputs) + list(scratch)
    in_hbm = [n.endswith("_hbm") or n == "base" for n in inputs]
    values = [
        pltpu.with_memory_space_constraint(v, pltpu.HBM) if n.endswith("_hbm") else v for n, v in operands.items()
    ]
    aliases = {inputs.index("base"): list(outputs).index("whole")} if "base" in inputs else {}
    results = pl.pallas_call(
        lambda *refs: kernel(dict(zip(names, refs))),
        out_shape=list(outputs.values()),
        in_specs=[HBM if there else VMEM for there in in_hbm],
        out_specs=[HBM if n in ("whole", "first_next", "second_next") else VMEM for n in outputs],
        input_output_aliases=aliases,
        scratch_shapes=list(scratch.values()),
        compiler_params=pltpu.CompilerParams(vmem_limit_bytes=22 << 20),
        cost_estimate=pl.CostEstimate(flops=flops, bytes_accessed=moved, transcendentals=0),
        name=kernel.__name__.removesuffix("_kernel"),
    )(*values)
    return dict(zip(outputs, results))


def shape(*dims):
    return jax.ShapeDtypeStruct(dims, BF16)


def flat(array):
    frames = array.shape[0]
    return array.transpose(0, 2, 1, 3).reshape(frames, MAIN, C)


def unflat(array):
    frames = array.shape[0]
    return array.reshape(frames, COLS, ROWS, C).transpose(0, 2, 1, 3)


def on_device(
    held_blocks,
    incoming,
    frame_counts,
    first_cache,
    second_cache,
    first_kernel,
    first_bias,
    first_gain,
    second_kernel,
    second_bias,
    second_gain,
):
    segments = lax.axis_size("segment")
    strips = lax.axis_size("strip")
    axes = ("segment", "strip")

    def swap(rows, far, step):
        pairs = []
        for s in range(segments):
            for k in range(strips):
                to, into = (((k + 1) ^ 1) - 1 if far else k ^ 1), (s + step) % segments
                if not 0 <= to < strips:
                    to, into = k, (into if step else s ^ 1)
                pairs.append((s * strips + k, into * strips + to))
        return lax.ppermute(rows, axes, pairs)

    x = flat(held_blocks[0])
    first = flat(first_cache[0])
    second = flat(second_cache[0])
    near, far = pl.pallas_call(
        pack_kernel,
        out_shape=[pltpu.VMEM((8, EDGE, C), BF16)] * 2,
        in_specs=[HBM] + [VMEM] * 3,
        out_specs=[VMEM] * 2,
        scratch_shapes=[pltpu.SMEM((9,), jnp.int32), pltpu.SemaphoreType.DMA],
        compiler_params=pltpu.CompilerParams(vmem_limit_bytes=8 << 20),
        name="pack",
    )(*(pltpu.with_memory_space_constraint(rows, pltpu.HBM) for rows in (frame_counts, x, first, second)))
    near, far = swap(near, False, 0), swap(far, True, 0)
    counts = dict(counts_hbm=frame_counts)
    count_scratch = dict(counts=pltpu.SMEM((9,), jnp.int32), sems=pltpu.SemaphoreType.DMA((16,)))
    block = pltpu.VMEM((FRAMES, MAIN, C), BF16)
    cached = pltpu.VMEM((2, MAIN, C), BF16)
    weights = pltpu.VMEM((3, K, C), BF16)
    ready = call(
        prepare_kernel,
        dict(
            x_hbm=x,
            first_hbm=first,
            second_hbm=second,
            incoming_hbm=flat(incoming[0]),
            bias1_hbm=first_bias,
            gain1_hbm=first_gain,
            bias2_hbm=second_bias,
            gain2_hbm=second_gain,
            weights1_hbm=first_kernel[0].reshape(3, K, C),
            **counts,
        ),
        dict(
            x=block,
            second=cached,
            incoming=block,
            window1=pltpu.VMEM(WINDOW, BF16),
            weights1=weights,
            **{n: pltpu.VMEM((1, C), F32) for n in VECTORS},
        ),
        count_scratch,
        moved=2 * 3 * K * C,
    )
    vectors = {n: ready[n] for n in VECTORS}
    done = call(
        tick0_kernel,
        dict(**counts, near=near, far=far, weights2_hbm=second_kernel[0].reshape(3, K, C), **ready),
        dict(
            weights2=weights,
            halos=pltpu.VMEM((FRAMES + 2, 2 * EDGE, C), BF16),
            window2=pltpu.VMEM(WINDOW, BF16),
            hidden_edges=pltpu.VMEM((FRAMES + 2, EDGE, C), F32),
            result=block,
            send=shape(FRAMES, MAIN, C),
            send_near=shape(FRAMES, EDGE, C),
            send_far=shape(FRAMES, EDGE, C),
        ),
        {**OPERANDS, **count_scratch},
    )

    onward = [(s * strips + k, (s + 1) % segments * strips + k) for s in range(segments) for k in range(strips)]
    x = lax.ppermute(done["send"], axes, onward)
    near, far = swap(done["send_near"], False, 1), swap(done["send_far"], True, 1)
    both = dict(weights1=ready["weights1"], weights2=done["weights2"])
    early = call(
        between_kernel,
        dict(
            **counts,
            window1_old=ready["window1"],
            halos_old=done["halos"],
            window2_old=done["window2"],
            edges_old=done["hidden_edges"],
            result=done["result"],
            **both,
        ),
        dict(
            whole=shape(2, FRAMES, MAIN, C),
            first=cached,
            first_halo=pltpu.VMEM((2, 2 * EDGE, C), BF16),
            second=cached,
            second_edge=pltpu.VMEM((2, EDGE, C), F32),
            sum1=pltpu.VMEM((2, MAIN, C), F32),
            sum_edges=pltpu.VMEM((2 * EDGE, C), F32),
            sum2=pltpu.VMEM((2, MAIN, C), F32),
        ),
        {**OPERANDS, **count_scratch},
        flops=2 * 2 * 3 * MAIN * K * C,
        moved=2 * 3 * K * C,
    )
    whole = early.pop("whole")
    for name, sums in (("early1", "sum1"), ("early_edges", "sum_edges"), ("early2", "sum2")):
        early[name] = early.pop(sums)
    out = call(
        tick1_kernel,
        dict(**counts, x=x, near=near, far=far, **early, **both, **vectors, base=whole),
        dict(whole=shape(2, FRAMES, MAIN, C), first_next=shape(2, MAIN, C), second_next=shape(2, MAIN, C)),
        dict(
            window1=pltpu.VMEM(WINDOW, BF16),
            halos=pltpu.VMEM((FRAMES + 2, 2 * EDGE, C), BF16),
            window2=pltpu.VMEM(WINDOW, BF16),
            hidden_edges=pltpu.VMEM((FRAMES + 2, EDGE, C), F32),
            result=block,
            **OPERANDS,
            **count_scratch,
        ),
    )
    return (
        unflat(out["whole"].reshape(2 * FRAMES, MAIN, C)).reshape(2, 1, FRAMES, ROWS, COLS, C),
        unflat(out["first_next"])[None],
        unflat(out["second_next"])[None],
    )


def solution(mesh):
    return jax.shard_map(
        on_device,
        mesh=mesh,
        in_specs=(
            P("segment", None, "strip", None, None),
            P(None, None, "strip", None, None),
            P(),
            P("segment", None, "strip", None, None),
            P("segment", None, "strip", None, None),
            P("segment", None, None, None, None, None),
            P("segment", None),
            P("segment", None),
            P("segment", None, None, None, None, None),
            P("segment", None),
            P("segment", None),
        ),
        out_specs=(
            P(None, "segment", None, "strip", None, None),
            P("segment", None, "strip", None, None),
            P("segment", None, "strip", None, None),
        ),
        check_vma=False,
    )
```

```python
import jax
import jax.numpy as jnp
from jax import lax
from jax.experimental import pallas as pl
from jax.experimental.pallas import tpu as pltpu
from jax.sharding import PartitionSpec as P

EPSILON = 1e-06
C = 384
FRAMES = 4
COLS = 12
ROWS = 8
MAIN = COLS * ROWS
EDGE = COLS * 2
TAPS = 9
K = TAPS * C
TILE = 256
STEPS = -(-K // TILE)
BF16 = jnp.bfloat16
F32 = jnp.float32
VMEM = pl.BlockSpec(memory_space=pltpu.VMEM)
HBM = pl.BlockSpec(memory_space=pltpu.HBM)


def rolled(value, shift, axis):
    shift = shift % value.shape[axis]
    return pltpu.roll(value, shift, axis) if shift else value


def rows_out(main, first):
    split = main.reshape(3, 4, ROWS, C)
    group = lax.broadcasted_iota(jnp.int32, (3, ROWS, C), 1) // 2
    out = None
    for q in range(4):
        piece = rolled(split[:, q], 2 * q - first, 1)
        out = piece if out is None else jnp.where(group == q, piece, out)
    return out.reshape(EDGE, C)


def spread(edge, which, to):
    split = edge.reshape(3, ROWS, C)
    pieces = [rolled(split, to - (2 * q + which), 1) for q in range(4)]
    return jnp.stack(pieces, axis=1).reshape(COLS, ROWS, C)


def shifted_row(main, b, before, before_which, after, after_which):
    if b == 1:
        return main
    split = main.reshape(COLS, ROWS, C)
    place = lax.broadcasted_iota(jnp.int32, (COLS, ROWS, C), 1)
    if b == 0:
        moved = jnp.where(place == 0, spread(before, before_which, 0), rolled(split, 1, 1))
    else:
        moved = jnp.where(place == ROWS - 1, spread(after, after_which, ROWS - 1), rolled(split, -1, 1))
    return moved.reshape(MAIN, C)


def column_taps(main):
    zeros = jnp.zeros((ROWS, C), F32)
    return [
        jnp.concatenate([zeros, main[: MAIN - ROWS]], axis=0),
        main,
        jnp.concatenate([main[ROWS:], zeros], axis=0),
    ]


def edge_column_taps(edge):
    place = lax.broadcasted_iota(jnp.int32, (EDGE, C), 0)
    return [
        jnp.where(place < 2, 0.0, rolled(edge, 2, 0)),
        edge,
        jnp.where(place >= EDGE - 2, 0.0, rolled(edge, -2, 0)),
    ]


def merged(even, odd):
    return jnp.where(lax.broadcasted_iota(jnp.int32, (EDGE, C), 0) % 2 == 0, even, odd)


def edge_pair(top, bottom):
    return merged(rolled(top, -1, 0), rolled(bottom, 1, 0))


def normed(values, gain):
    factor = lax.rsqrt(jnp.mean(values * values, axis=-1, keepdims=True) + EPSILON)
    v = values * factor * gain
    return v / (1.0 + jnp.exp(-v))


def weight_tile(weights, taps, step):
    at = step * TILE
    depth = min(TILE, K - at)
    if len(taps) == 1:
        tile = weights[taps[0]][at : at + depth, 0:TILE]
    else:
        empty = jnp.zeros((depth, C - TILE), BF16)
        tile = jnp.concatenate(
            [empty if a is None else weights[a][at : at + depth, TILE:C] for a in taps], axis=1
        )
    if depth < TILE:
        tile = jnp.concatenate([tile, jnp.zeros((TILE - depth, TILE), BF16)], axis=0)
    return tile


def multiply(accumulator, operand, index, step, slot):
    at = step * TILE
    depth = min(TILE, K - at)
    rows = operand[index, :, at : at + depth]
    if depth < TILE:
        rows = jnp.concatenate([rows, rows], axis=1)
    pltpu.matmul_acc_lhs(accumulator, rows, load_staged_rhs=slot)


def halves(accumulator):
    both = pltpu.matmul_pop(accumulator)
    return both[:, : C - TILE], both[:, C - TILE :]


def timeline(phases, groups):
    clock, starts, ends, entries = [0, 0], {}, {}, []
    for name, units in phases:
        for unit, steps in enumerate(units):
            starts[name, unit] = clock[unit]
            for step in steps:
                entries.append((clock[unit], 1, len(entries), step))
                clock[unit] += sum(operand.shape[1] for _, operand, _ in step[4])
            ends[name, unit] = clock[unit]
    for after, before, thunks in groups:
        first = max(ends[after, 0], ends[after, 1]) if after else -1
        last = min(starts[before, 0], starts[before, 1]) if before else max(clock) + 1
        last = max(last, first + 0.5)
        for i, thunk in enumerate(thunks):
            entries.append((first + (last - first) * i / len(thunks), 0, len(entries), thunk))
    return [entry[3] for entry in sorted(entries, key=lambda entry: entry[:3])]


def first_normed(frame, keep, gain):
    return normed(jnp.where(keep, frame.astype(F32), 0.0), gain).astype(BF16)


class Section:
    def __init__(self, refs, accumulators, even, at_top, at_bottom):
        self.__dict__.update(refs)
        self.even, self.at_top, self.at_bottom = even, at_top, at_bottom
        at = 0
        for name, (_, _, count) in ACCUMULATORS.items():
            setattr(self, name, accumulators[at : at + count])
            at += count
        self.left = [self.left[:4], self.left[:2] + self.left[4:]]
        self.right = [self.right[:5], self.right[:3] + self.right[5:] + self.right[4:5]]
        self.saved = None

    def halo(self, f):
        near, far = self.near[f].astype(F32), self.far[f].astype(F32)
        top = jnp.where(self.at_top, 0.0, jnp.where(self.even, far, near))
        bottom = jnp.where(self.at_bottom, 0.0, jnp.where(self.even, near, far))
        return top, bottom

    def norm_first(self, f):
        self.window1[f + 2] = normed(self.x[f].astype(F32), self.gain1[...]).astype(BF16)

    def norm_first_halo(self, f):
        gain = self.gain1[...]
        values = jnp.concatenate(self.halo(f), axis=0)
        if not self.norms:
            values = jnp.where(f < self.live(), values, 0.0)
        self.halos[f + 2] = normed(values, gain).astype(BF16)

    def build_first_edges(self, g):
        main = self.window1[g].astype(F32)
        halo = self.halos[g].astype(F32)
        top, bottom = halo[:EDGE], halo[EDGE:]
        even = lax.broadcasted_iota(jnp.int32, (EDGE, C), 0) % 2 == 0
        self.edge_rows[g, 0] = jnp.where(even, top, rows_out(main, 6))
        self.edge_rows[g, 1] = edge_pair(top, bottom)
        self.edge_rows[g, 2] = jnp.where(even, rows_out(main, 0), bottom)

    def build_first_pair(self, g, b):
        taps = [edge_column_taps(self.edge_rows[g + i, b]) for i in range(2)]
        for c in range(3):
            at = (3 * b + c) * C
            rows = jnp.concatenate([taps[0][c], taps[1][c]], axis=0)
            self.edges[g, :, at : at + C] = rows.astype(BF16)

    def build_first(self, g, b):
        main = self.window1[g].astype(F32)
        halo = self.halos[g].astype(F32)
        self.build(self.operand1, g, b, main, halo[:EDGE], 1, halo[EDGE:], 0)

    def build_second(self, g, b):
        main = self.window2[g].astype(F32)
        edge = self.hidden_edges[g]
        self.build(self.operand2, g, b, main, edge, 0, edge, 1)

    def build(self, operand, g, b, main, before, before_which, after, after_which):
        rows = shifted_row(main, b, before, before_which, after, after_which)
        for c, taps in enumerate(column_taps(rows)):
            at = (3 * b + c) * C
            operand[g, :, at : at + C] = taps.astype(BF16)

    def first_thunks(self, pair, cached=False):
        out = []
        for g in (pair, pair + 1):
            if not cached:
                out += [lambda f=g - 2: self.norm_first(f)] if self.norms else []
                out += [lambda f=g - 2: self.norm_first_halo(f)]
        for g in (pair, pair + 1):
            out += [lambda g=g: self.build_first_edges(g)]
            out += [lambda g=g, b=b: self.build_first(g, b) for b in range(3)]
        starts = [pair] if pair == 0 else [pair - 1, pair]
        out += [lambda g=g, b=b: self.build_first_pair(g, b) for g in starts for b in range(3)]
        return out

    def second_thunks(self, pair, cached=False):
        out = []
        if not cached:
            out += [lambda f=f: self.norm_second(f) for f in (pair - 2, pair - 1)]
            out += [lambda i=pair // 2 - 1: self.norm_second_edges(i)]
        out += [lambda g=g, b=b: self.build_second(g, b) for g in (pair, pair + 1) for b in range(3)]
        return out

    def pop_sums(self, conv, f):
        left = pltpu.matmul_pop(self.left[conv][f])
        if f < 2 and conv in self.moved:
            left = left + pltpu.matmul_pop(self.moved_left[f])
        if f == 0:
            self.saved = halves(self.right[conv][0])[0] if self.early1 is None else 0.0
        right, (following, second) = self.saved, halves(self.right[conv][f + 1])
        self.saved = following
        sums = jnp.concatenate([left, right + second], axis=1)
        if self.early1 is not None and f < 2:
            sums = sums + (self.early1, self.early2)[conv][f]
        return sums

    def pop_edges(self, i):
        left = pltpu.matmul_pop(self.left_edges[i])
        if i == 0 and 0 in self.moved:
            left = left + pltpu.matmul_pop(self.moved_edges[0])
        if i or self.early1 is None:
            right = halves(self.right_edges[i])[0] + halves(self.right_edges[2 + i])[1]
        else:
            right = halves(self.right_edges[2])[1]
        sums = jnp.concatenate([left, right], axis=1)
        return sums + self.early_edges[...] if self.early1 is not None and i == 0 else sums

    def norm_second(self, f):
        hidden = jnp.where(f < self.live(), self.pop_sums(0, f) + self.bias1[...], 0.0)
        self.window2[f + 2] = normed(hidden, self.gain2[...]).astype(BF16)

    def norm_second_edges(self, i):
        hidden = self.pop_edges(i) + self.bias1[...]
        place = lax.broadcasted_iota(jnp.int32, (2 * EDGE, C), 0)
        outside = ((place % 2 == 0) & self.at_top) | ((place % 2 == 1) & self.at_bottom)
        hidden = jnp.where(outside, 0.0, hidden)
        values = normed(hidden, self.gain2[...]).astype(BF16).astype(F32)
        for j in range(2):
            f = 2 * i + j
            self.hidden_edges[f + 2] = jnp.where(f < self.live(), values[j * EDGE : (j + 1) * EDGE], 0.0)

    def final(self, f):
        result = self.pop_sums(1, f) + self.bias2[...] + self.x[f].astype(F32)
        return jnp.where(f < self.live(), result, 0.0).astype(BF16)

    def phase(self, conv, pair):
        if conv == 0:
            weights = [self.weights1.at[0], self.weights1.at[1], self.weights1_last]
        else:
            weights = [self.weights2.at[a] for a in range(3)]
        operand = (self.operand1, self.operand2)[conv]
        moved = conv in self.moved
        units = ([], [])

        def add(unit, taps, work, edge_work=()):
            work = [(accumulator, operand, g) for accumulator, g in work]
            if conv == 0:
                work += [(accumulator, self.edges, g) for accumulator, g in edge_work]
            units[unit].extend((unit, taps, step, weights, work) for step in range(STEPS))

        left, right = self.left[conv], self.right[conv]
        for a in range(3):
            work = [(left[g - a], g) for g in (pair, pair + 1) if 0 <= g - a < FRAMES]
            edge_work = [(self.left_edges[i], 2 * i + a) for i in range(2) if pair <= 2 * i + a + 1 < pair + 2]
            if work and not (moved and pair == 2 and a == 2):
                add(0, (a,), work, edge_work)
        edges = self.right_edges
        if pair == 0:
            add(1, (0, 1), [(right[0], 0), (right[1], 1)], [(edges[0], 0)])
        elif pair == 2:
            add(1, (0, 1), [(right[2], 2), (right[3], 3)], [(edges[2], 1), (edges[1], 2)])
            add(1, (None, 2), [(right[1], 2), (right[2], 3)], [(edges[2], 2)])
            if moved:
                add(1, (2,), [(self.moved_left[f], f + 2) for f in range(2)], [(self.moved_edges[0], 2)])
        else:
            add(1, (1, 2), [(right[3], 4), (right[4], 5)], [(edges[1], 3), (edges[3], 4)])
        return (conv, pair), units

    def run(self, order):
        steps = [[entry for entry in order if isinstance(entry, tuple) and entry[0] == unit] for unit in range(2)]
        count = [0, 0]

        def push(unit, i):
            _, taps, step, weights, _ = steps[unit][i]
            pltpu.matmul_push_rhs(weight_tile(weights, taps, step), i % 2, unit)

        for entry in order:
            if not isinstance(entry, tuple):
                entry()
                continue
            unit, _, step, _, work = entry
            i = count[unit]
            count[unit] += 1
            if i == 0:
                push(unit, 0)
            if i + 1 < len(steps[unit]):
                push(unit, i + 1)
            for n, (accumulator, operand, g) in enumerate(work):
                multiply(accumulator, operand, g, step, i % 2 if n == 0 else None)


def hand_out(upper, lower, even, near, far, f):
    near[f] = jnp.where(even, lower, upper).astype(BF16)
    far[f] = jnp.where(even, upper, lower).astype(BF16)


def edges_out(main, even, near, far, f):
    hand_out(rows_out(main, 0), rows_out(main, 6), even, near, far, f)


def pack_kernel(x, first, second, near, far):
    even = lax.axis_index("strip") % 2 == 0
    for source, start in ((first, 4), (x, 0)):
        for f in range(source.shape[0]):
            edges_out(source[f].astype(F32), even, near, far, start + f)
    frames = [second[f].astype(F32) for f in range(2)]
    upper, lower = ([rows_out(rows, at) for rows in frames] for at in (0, 6))
    upper = merged(upper[0], rolled(upper[1], 1, 0))
    lower = merged(rolled(lower[0], -1, 0), lower[1])
    hand_out(upper, lower, even, near, far, 6)


WINDOW = (FRAMES + 2, MAIN, C)
OPERANDS = dict(
    edge_rows=pltpu.VMEM((FRAMES + 2, 3, EDGE, C), F32),
    operand1=pltpu.VMEM((FRAMES + 2, MAIN, K), BF16),
    edges=pltpu.VMEM((FRAMES + 1, 2 * EDGE, K), BF16),
    operand2=pltpu.VMEM((FRAMES + 2, MAIN, K), BF16),
)
VECTORS = ("bias1", "gain1", "bias2", "gain2")


def live_frames(counts, tick):
    return counts[7 - lax.axis_index("segment") + tick]


ACCUMULATORS = dict(
    left=(0, MAIN, FRAMES + 2),
    left_edges=(0, 2 * EDGE, 2),
    right=(1, MAIN, FRAMES + 2),
    right_edges=(1, 2 * EDGE, 4),
    moved_left=(1, MAIN, 2),
    moved_edges=(1, 2 * EDGE, 1),
)


def with_section(given, body):
    strip = lax.axis_index("strip")
    given = {"early1": None, **given}

    def inner(*accumulators):
        body(Section(given, accumulators, strip % 2 == 0, strip == 0, strip == lax.axis_size("strip") - 1))

    shapes = [pltpu.ACC(unit)((rows, TILE), F32) for unit, rows, count in ACCUMULATORS.values() for _ in range(count)]
    pl.run_scoped(inner, *shapes)


def prepare_kernel(r):
    pairs = [(r[n + "_hbm"], r[n]) for n in ("x", "gain1", "bias1", "gain2", "bias2", "second", "incoming")]
    pairs += [(r["counts_hbm"], r["counts"]), (r["first_hbm"], r["window1"].at[pl.ds(0, 2)])]
    pairs += [(r["weights1_hbm"].at[a], r["weights1"].at[a]) for a in range(2)]
    copies = [pltpu.make_async_copy(source, target, r["sems"].at[i]) for i, (source, target) in enumerate(pairs)]
    for copy in copies:
        copy.start()
    copies[7].wait()
    copies[0].wait()
    copies[1].wait()
    live = live_frames(r["counts"], 0)
    gain = r["gain1"][...]
    for f in range(FRAMES):
        r["window1"][f + 2] = first_normed(r["x"][f], f < live, gain)
    for i, copy in enumerate(copies):
        if i not in (0, 1, 7):
            copy.wait()


def tick0_kernel(r):
    counting = pltpu.make_async_copy(r["counts_hbm"], r["counts"], r["sems"].at[3])
    counting.start()
    pairs = [(r["weights1_hbm"].at[2], r["weights1_last"])]
    pairs += [(r["weights2_hbm"].at[a], r["weights2"].at[a]) for a in range(3)]
    copies = [pltpu.make_async_copy(source, target, r["sems"].at[4 + i]) for i, (source, target) in enumerate(pairs)]
    for copy in copies:
        copy.start()

    def body(work):
        work.norms = False
        work.moved = (0, 1)
        work.live = lambda: live_frames(r["counts"], 0)
        work.window2[0:2] = work.second[...]
        for g in range(2):
            work.halos[g] = jnp.concatenate(work.halo(4 + g), axis=0).astype(BF16)
        top, bottom = work.halo(6)
        work.hidden_edges[0] = merged(top, rolled(bottom, 1, 0))
        work.hidden_edges[1] = merged(rolled(top, -1, 0), bottom)
        last = lax.axis_index("segment") == lax.axis_size("segment") - 1

        def finish(f):
            result = work.final(f)
            work.result[f] = result
            fresh = jnp.where(f < r["counts"][8], work.incoming[f].astype(F32), 0.0)
            passed = jnp.where(last, fresh, result.astype(F32))
            work.send[f] = passed.astype(BF16)
            edges_out(passed, work.even, work.send_near, work.send_far, f)

        finishing = [lambda f=f: finish(f) for f in range(FRAMES)]
        phases = [work.phase(conv, pair) for conv in range(2) for pair in (0, 2, 4)]
        groups = [
            (None, (0, 2), work.first_thunks(2)),
            ((0, 0), (0, 4), work.first_thunks(4)),
            ((0, 0), (0, 4), work.second_thunks(0, cached=True)),
            ((0, 0), (0, 4), [copies[0].wait]),
            ((0, 2), (1, 0), [copy.wait for copy in copies[1:]]),
            ((0, 2), (1, 0), work.second_thunks(2)),
            ((0, 4), (1, 2), work.second_thunks(4)),
            ((1, 2), None, finishing[:2]),
        ]
        order = work.first_thunks(0, cached=True) + [counting.wait] + timeline(phases, groups)
        work.run(order + finishing[2:])

    with_section(r, body)


def between_kernel(r):
    writing = pltpu.make_async_copy(r["result"], r["whole"].at[0], r["sems"].at[0])
    writing.start()
    counting = pltpu.make_async_copy(r["counts_hbm"], r["counts"], r["sems"].at[1])
    counting.start()
    counting.wait()
    live = live_frames(r["counts"], 0)
    for i in range(2):
        r["first"][i] = r["window1_old"][live + i]
        r["first_halo"][i] = r["halos_old"][live + i]
        r["second"][i] = r["window2_old"][live + i]
        r["second_edge"][i] = r["edges_old"][live + i]

    def body(work):
        work.moved = ()

        def store(conv, sums):
            for f in range(2):
                right, second = halves(work.right[conv][f])
                if f == 1:
                    sums[0, :, TILE:C] += second
                sums[f, :, 0:TILE] = pltpu.matmul_pop(work.left[conv][f])
                sums[f, :, TILE:C] = right
            if conv == 0:
                work.sum_edges[:, 0:TILE] = pltpu.matmul_pop(work.left_edges[0])
                work.sum_edges[:, TILE:C] = halves(work.right_edges[0])[0]

        order = work.first_thunks(0, cached=True)
        order += timeline([work.phase(0, 0)], [(None, None, work.second_thunks(0, cached=True))])
        order += [lambda: store(0, work.sum1)]
        order += timeline([work.phase(1, 0)], [])
        work.run(order)
        store(1, work.sum2)

    given = dict(r, window1=r["first"], halos=r["first_halo"], window2=r["second"], hidden_edges=r["second_edge"])
    with_section(given, body)
    writing.wait()


def tick1_kernel(r):
    counting = pltpu.make_async_copy(r["counts_hbm"], r["counts"], r["sems"].at[0])
    counting.start()
    copies = []

    def send(source, target):
        copies.append(pltpu.make_async_copy(source, target, r["sems"].at[len(copies) + 1]))
        copies[-1].start()

    def body(work):
        work.norms = True
        work.moved = (1,)
        work.live = lambda: live_frames(r["counts"], 1)
        for i in range(2):
            work.window1[i] = work.first[i]
            work.halos[i] = work.first_halo[i]
            work.window2[i] = work.second[i]
            work.hidden_edges[i] = work.second_edge[i]

        def finish(f):
            work.result[f] = work.final(f)
            send(work.result.at[f], work.whole.at[1, f])

        def send_window(window, target):
            send(window.at[pl.ds(work.live(), 2)], target)

        finishing = [lambda f=f: finish(f) for f in range(FRAMES)]
        phases = [work.phase(conv, pair) for conv in range(2) for pair in (2, 4)]
        groups = [
            (None, (0, 4), work.first_thunks(4)),
            (None, (0, 4), [counting.wait]),
            ((0, 2), (1, 2), work.second_thunks(2)),
            ((0, 2), (1, 2), [lambda: send_window(work.window1, work.first_next)]),
            ((0, 4), (1, 4), work.second_thunks(4)),
            ((1, 2), None, finishing[:2]),
        ]
        order = [lambda: work.build_first_edges(1)] + work.first_thunks(2) + timeline(phases, groups)
        work.run(order + [lambda: send_window(work.window2, work.second_next)] + finishing[2:])
        for copy in copies:
            copy.wait()

    with_section(r, body)


def call(kernel, operands, outputs, scratch, flops=0, moved=0):
    inputs = list(operands)
    names = inputs + list(outputs) + list(scratch)
    in_hbm = [n.endswith("_hbm") or n == "base" for n in inputs]
    values = [
        pltpu.with_memory_space_constraint(v, pltpu.HBM) if n.endswith("_hbm") else v for n, v in operands.items()
    ]
    aliases = {inputs.index("base"): list(outputs).index("whole")} if "base" in inputs else {}
    results = pl.pallas_call(
        lambda *refs: kernel(dict(zip(names, refs))),
        out_shape=list(outputs.values()),
        in_specs=[HBM if there else VMEM for there in in_hbm],
        out_specs=[HBM if n in ("whole", "first_next", "second_next") else VMEM for n in outputs],
        input_output_aliases=aliases,
        scratch_shapes=list(scratch.values()),
        compiler_params=pltpu.CompilerParams(vmem_limit_bytes=22 << 20),
        cost_estimate=pl.CostEstimate(flops=flops, bytes_accessed=moved, transcendentals=0),
        name=kernel.__name__.removesuffix("_kernel"),
    )(*values)
    return dict(zip(outputs, results))


def shape(*dims):
    return jax.ShapeDtypeStruct(dims, BF16)


def flat(array):
    frames = array.shape[0]
    return array.transpose(0, 2, 1, 3).reshape(frames, MAIN, C)


def unflat(array):
    frames = array.shape[0]
    return array.reshape(frames, COLS, ROWS, C).transpose(0, 2, 1, 3)


def on_device(
    held_blocks,
    incoming,
    frame_counts,
    first_cache,
    second_cache,
    first_kernel,
    first_bias,
    first_gain,
    second_kernel,
    second_bias,
    second_gain,
):
    segments = lax.axis_size("segment")
    strips = lax.axis_size("strip")
    axes = ("segment", "strip")

    def swap(rows, far, step):
        pairs = []
        for s in range(segments):
            for k in range(strips):
                to, into = (((k + 1) ^ 1) - 1 if far else k ^ 1), (s + step) % segments
                if not 0 <= to < strips:
                    to, into = k, (into if step else s ^ 1)
                pairs.append((s * strips + k, into * strips + to))
        return lax.ppermute(rows, axes, pairs)

    x = flat(held_blocks[0])
    first = flat(first_cache[0])
    second = flat(second_cache[0])
    near, far = pl.pallas_call(
        pack_kernel,
        out_shape=[pltpu.VMEM((7, EDGE, C), BF16)] * 2,
        in_specs=[VMEM] * 3,
        out_specs=[VMEM] * 2,
        compiler_params=pltpu.CompilerParams(vmem_limit_bytes=8 << 20),
        name="pack",
    )(*(pltpu.with_memory_space_constraint(rows, pltpu.HBM) for rows in (x, first, second)))
    far = swap(far, True, 0)
    near = swap(near, False, 0)
    counts = dict(counts_hbm=frame_counts)
    count_scratch = dict(counts=pltpu.SMEM((9,), jnp.int32), sems=pltpu.SemaphoreType.DMA((16,)))
    block = pltpu.VMEM((FRAMES, MAIN, C), BF16)
    cached = pltpu.VMEM((2, MAIN, C), BF16)
    weights = pltpu.VMEM((3, K, C), BF16)
    ready = call(
        prepare_kernel,
        dict(
            x_hbm=x,
            first_hbm=first,
            second_hbm=second,
            incoming_hbm=flat(incoming[0]),
            bias1_hbm=first_bias,
            gain1_hbm=first_gain,
            bias2_hbm=second_bias,
            gain2_hbm=second_gain,
            weights1_hbm=first_kernel[0].reshape(3, K, C),
            **counts,
        ),
        dict(
            x=block,
            second=cached,
            incoming=block,
            window1=pltpu.VMEM(WINDOW, BF16),
            weights1=pltpu.VMEM((2, K, C), BF16),
            **{n: pltpu.VMEM((1, C), F32) for n in VECTORS},
        ),
        count_scratch,
        moved=2 * 2 * K * C,
    )
    vectors = {n: ready[n] for n in VECTORS}
    done = call(
        tick0_kernel,
        dict(
            **counts,
            far=far,
            near=near,
            weights1_hbm=first_kernel[0].reshape(3, K, C),
            weights2_hbm=second_kernel[0].reshape(3, K, C),
            **ready,
        ),
        dict(
            weights1_last=pltpu.VMEM((K, C), BF16),
            weights2=weights,
            halos=pltpu.VMEM((FRAMES + 2, 2 * EDGE, C), BF16),
            window2=pltpu.VMEM(WINDOW, BF16),
            hidden_edges=pltpu.VMEM((FRAMES + 2, EDGE, C), F32),
            result=block,
            send=shape(FRAMES, MAIN, C),
            send_near=shape(FRAMES, EDGE, C),
            send_far=shape(FRAMES, EDGE, C),
        ),
        {**OPERANDS, **count_scratch},
    )

    onward = [(s * strips + k, (s + 1) % segments * strips + k) for s in range(segments) for k in range(strips)]
    far = swap(done["send_far"], True, 1)
    near = swap(done["send_near"], False, 1)
    x = lax.ppermute(done["send"], axes, onward)
    both = dict(weights1=ready["weights1"], **{n: done[n] for n in ("weights1_last", "weights2")})
    early = call(
        between_kernel,
        dict(
            **counts,
            window1_old=ready["window1"],
            halos_old=done["halos"],
            window2_old=done["window2"],
            edges_old=done["hidden_edges"],
            result=done["result"],
            **both,
        ),
        dict(
            whole=shape(2, FRAMES, MAIN, C),
            first=cached,
            first_halo=pltpu.VMEM((2, 2 * EDGE, C), BF16),
            second=cached,
            second_edge=pltpu.VMEM((2, EDGE, C), F32),
            sum1=pltpu.VMEM((2, MAIN, C), F32),
            sum_edges=pltpu.VMEM((2 * EDGE, C), F32),
            sum2=pltpu.VMEM((2, MAIN, C), F32),
        ),
        {**OPERANDS, **count_scratch},
        flops=2 * 2 * 3 * MAIN * K * C,
        moved=2 * 3 * K * C,
    )
    whole = early.pop("whole")
    for name, sums in (("early1", "sum1"), ("early_edges", "sum_edges"), ("early2", "sum2")):
        early[name] = early.pop(sums)
    out = call(
        tick1_kernel,
        dict(**counts, far=far, near=near, x=x, **early, **both, **vectors, base=whole),
        dict(whole=shape(2, FRAMES, MAIN, C), first_next=shape(2, MAIN, C), second_next=shape(2, MAIN, C)),
        dict(
            window1=pltpu.VMEM(WINDOW, BF16),
            halos=pltpu.VMEM((FRAMES + 2, 2 * EDGE, C), BF16),
            window2=pltpu.VMEM(WINDOW, BF16),
            hidden_edges=pltpu.VMEM((FRAMES + 2, EDGE, C), F32),
            result=block,
            **OPERANDS,
            **count_scratch,
        ),
    )
    return (
        unflat(out["whole"].reshape(2 * FRAMES, MAIN, C)).reshape(2, 1, FRAMES, ROWS, COLS, C),
        unflat(out["first_next"])[None],
        unflat(out["second_next"])[None],
    )


def solution(mesh):
    return jax.shard_map(
        on_device,
        mesh=mesh,
        in_specs=(
            P("segment", None, "strip", None, None),
            P(None, None, "strip", None, None),
            P(),
            P("segment", None, "strip", None, None),
            P("segment", None, "strip", None, None),
            P("segment", None, None, None, None, None),
            P("segment", None),
            P("segment", None),
            P("segment", None, None, None, None, None),
            P("segment", None),
            P("segment", None),
        ),
        out_specs=(
            P(None, "segment", None, "strip", None, None),
            P("segment", None, "strip", None, None),
            P("segment", None, "strip", None, None),
        ),
        check_vma=False,
    )
```

```python
import jax
import jax.numpy as jnp
from jax import lax
from jax.experimental import pallas as pl
from jax.experimental.pallas import tpu as pltpu
from jax.sharding import PartitionSpec as P

EPSILON = 1e-06
C = 384
FRAMES = 4
COLS = 12
ROWS = 8
MAIN = COLS * ROWS
EDGE = COLS * 2
TAPS = 9
K = TAPS * C
TILE = 256
STEPS = -(-K // TILE)
BF16 = jnp.bfloat16
F32 = jnp.float32
VMEM = pl.BlockSpec(memory_space=pltpu.VMEM)
HBM = pl.BlockSpec(memory_space=pltpu.HBM)


def rolled(value, shift, axis):
    shift = shift % value.shape[axis]
    return pltpu.roll(value, shift, axis) if shift else value


def rows_out(main, first):
    split = main.reshape(3, 4, ROWS, C)
    group = lax.broadcasted_iota(jnp.int32, (3, ROWS, C), 1) // 2
    out = None
    for q in range(4):
        piece = rolled(split[:, q], 2 * q - first, 1)
        out = piece if out is None else jnp.where(group == q, piece, out)
    return out.reshape(EDGE, C)


def spread(edge, which, to):
    split = edge.reshape(3, ROWS, C)
    pieces = [rolled(split, to - (2 * q + which), 1) for q in range(4)]
    return jnp.stack(pieces, axis=1).reshape(COLS, ROWS, C)


def shifted_row(main, b, before, before_which, after, after_which):
    if b == 1:
        return main
    split = main.reshape(COLS, ROWS, C)
    place = lax.broadcasted_iota(jnp.int32, (COLS, ROWS, C), 1)
    if b == 0:
        moved = jnp.where(place == 0, spread(before, before_which, 0), rolled(split, 1, 1))
    else:
        moved = jnp.where(place == ROWS - 1, spread(after, after_which, ROWS - 1), rolled(split, -1, 1))
    return moved.reshape(MAIN, C)


def column_taps(main):
    zeros = jnp.zeros((ROWS, C), F32)
    return [
        jnp.concatenate([zeros, main[: MAIN - ROWS]], axis=0),
        main,
        jnp.concatenate([main[ROWS:], zeros], axis=0),
    ]


def edge_column_taps(edge):
    place = lax.broadcasted_iota(jnp.int32, (EDGE, C), 0)
    return [
        jnp.where(place < 2, 0.0, rolled(edge, 2, 0)),
        edge,
        jnp.where(place >= EDGE - 2, 0.0, rolled(edge, -2, 0)),
    ]


def merged(even, odd):
    return jnp.where(lax.broadcasted_iota(jnp.int32, (EDGE, C), 0) % 2 == 0, even, odd)


def edge_pair(top, bottom):
    return merged(rolled(top, -1, 0), rolled(bottom, 1, 0))


def normed(values, gain):
    factor = lax.rsqrt(jnp.mean(values * values, axis=-1, keepdims=True) + EPSILON)
    v = values * factor * gain
    return v / (1.0 + jnp.exp(-v))


def weight_tile(weights, taps, step):
    at = step * TILE
    depth = min(TILE, K - at)
    if len(taps) == 1:
        tile = weights[taps[0]][at : at + depth, 0:TILE]
    else:
        empty = jnp.zeros((depth, C - TILE), BF16)
        tile = jnp.concatenate(
            [empty if a is None else weights[a][at : at + depth, TILE:C] for a in taps], axis=1
        )
    if depth < TILE:
        tile = jnp.concatenate([tile, jnp.zeros((TILE - depth, TILE), BF16)], axis=0)
    return tile


def multiply(accumulator, operand, index, step, slot):
    at = step * TILE
    depth = min(TILE, K - at)
    rows = operand[index, :, at : at + depth]
    if depth < TILE:
        rows = jnp.concatenate([rows, rows], axis=1)
    pltpu.matmul_acc_lhs(accumulator, rows, load_staged_rhs=slot)


def halves(accumulator):
    both = pltpu.matmul_pop(accumulator)
    return both[:, : C - TILE], both[:, C - TILE :]


def timeline(phases, groups):
    clock, starts, ends, entries = [0, 0], {}, {}, []
    for name, units in phases:
        for unit, steps in enumerate(units):
            starts[name, unit] = clock[unit]
            for step in steps:
                entries.append((clock[unit], 1, len(entries), step))
                clock[unit] += sum(operand.shape[1] for _, operand, _ in step[4])
            ends[name, unit] = clock[unit]
    for after, before, thunks in groups:
        first = max(ends[after, 0], ends[after, 1]) if isinstance(after, tuple) else after
        last = min(starts[before, 0], starts[before, 1]) if before else max(clock) + 1
        last = max(last, first + 0.5)
        for i, thunk in enumerate(thunks):
            entries.append((first + (last - first) * i / len(thunks), 0, len(entries), thunk))
    return [entry[3] for entry in sorted(entries, key=lambda entry: entry[:3])]


def first_normed(frame, keep, gain):
    return normed(jnp.where(keep, frame.astype(F32), 0.0), gain).astype(BF16)


class Section:
    def __init__(self, refs, accumulators, even, at_top, at_bottom):
        self.__dict__.update(refs)
        self.even, self.at_top, self.at_bottom = even, at_top, at_bottom
        at = 0
        for name, (_, _, count) in ACCUMULATORS.items():
            setattr(self, name, accumulators[at : at + count])
            at += count
        self.left = [self.left[:4], self.left[:2] + self.left[4:]]
        self.right = [self.right[:5], self.right[:3] + self.right[5:] + self.right[4:5]]
        self.saved = None

    def halo(self, f):
        near, far = self.near[f].astype(F32), self.far[f].astype(F32)
        top = jnp.where(self.at_top, 0.0, jnp.where(self.even, far, near))
        bottom = jnp.where(self.at_bottom, 0.0, jnp.where(self.even, near, far))
        return top, bottom

    def norm_first(self, f):
        self.window1[f + 2] = normed(self.x[f].astype(F32), self.gain1[...]).astype(BF16)

    def norm_first_halo(self, f):
        gain = self.gain1[...]
        values = jnp.concatenate(self.halo(f), axis=0)
        if not self.norms:
            values = jnp.where(f < self.live(), values, 0.0)
        self.halos[f + 2] = normed(values, gain).astype(BF16)

    def build_first_edges(self, g):
        main = self.window1[g].astype(F32)
        halo = self.halos[g].astype(F32)
        top, bottom = halo[:EDGE], halo[EDGE:]
        even = lax.broadcasted_iota(jnp.int32, (EDGE, C), 0) % 2 == 0
        self.edge_rows[g, 0] = jnp.where(even, top, rows_out(main, 6))
        self.edge_rows[g, 1] = edge_pair(top, bottom)
        self.edge_rows[g, 2] = jnp.where(even, rows_out(main, 0), bottom)

    def build_first_pair(self, g, b):
        taps = [edge_column_taps(self.edge_rows[g + i, b]) for i in range(2)]
        for c in range(3):
            at = (3 * b + c) * C
            rows = jnp.concatenate([taps[0][c], taps[1][c]], axis=0)
            self.edges[g, :, at : at + C] = rows.astype(BF16)

    def build_first(self, g, b):
        main = self.window1[g].astype(F32)
        halo = self.halos[g].astype(F32)
        self.build(self.operand1, g, b, main, halo[:EDGE], 1, halo[EDGE:], 0)

    def build_second(self, g, b):
        main = self.window2[g].astype(F32)
        edge = self.hidden_edges[g]
        self.build(self.operand2, g, b, main, edge, 0, edge, 1)

    def build(self, operand, g, b, main, before, before_which, after, after_which):
        rows = shifted_row(main, b, before, before_which, after, after_which)
        for c, taps in enumerate(column_taps(rows)):
            at = (3 * b + c) * C
            operand[g, :, at : at + C] = taps.astype(BF16)

    def first_thunks(self, pair, cached=False):
        out = []
        for g in (pair, pair + 1):
            if not cached:
                out += [lambda f=g - 2: self.norm_first(f)] if self.norms else []
                out += [lambda f=g - 2: self.norm_first_halo(f)]
        for g in (pair, pair + 1):
            out += [lambda g=g: self.build_first_edges(g)]
            out += [lambda g=g, b=b: self.build_first(g, b) for b in range(3)]
        starts = [pair] if pair == 0 else [pair - 1, pair]
        out += [lambda g=g, b=b: self.build_first_pair(g, b) for g in starts for b in range(3)]
        return out

    def second_thunks(self, pair, cached=False):
        out = []
        if not cached:
            out += [lambda f=f: self.norm_second(f) for f in (pair - 2, pair - 1)]
            out += [lambda i=pair // 2 - 1: self.norm_second_edges(i)]
        out += [lambda g=g, b=b: self.build_second(g, b) for g in (pair, pair + 1) for b in range(3)]
        return out

    def pop_sums(self, conv, f):
        left = pltpu.matmul_pop(self.left[conv][f])
        if f < 2 and conv in self.moved:
            left = left + pltpu.matmul_pop(self.moved_left[f])
        if f == 0:
            self.saved = halves(self.right[conv][0])[0] if self.early1 is None else 0.0
        right, (following, second) = self.saved, halves(self.right[conv][f + 1])
        self.saved = following
        sums = jnp.concatenate([left, right + second], axis=1)
        if self.early1 is not None and f < 2:
            sums = sums + (self.early1, self.early2)[conv][f]
        return sums

    def pop_edges(self, i):
        left = pltpu.matmul_pop(self.left_edges[i])
        if i == 0 and 0 in self.moved:
            left = left + pltpu.matmul_pop(self.moved_edges[0])
        if i or self.early1 is None:
            right = halves(self.right_edges[i])[0] + halves(self.right_edges[2 + i])[1]
        else:
            right = halves(self.right_edges[2])[1]
        sums = jnp.concatenate([left, right], axis=1)
        return sums + self.early_edges[...] if self.early1 is not None and i == 0 else sums

    def norm_second(self, f):
        hidden = jnp.where(f < self.live(), self.pop_sums(0, f) + self.bias1[...], 0.0)
        self.window2[f + 2] = normed(hidden, self.gain2[...]).astype(BF16)

    def norm_second_edges(self, i):
        hidden = self.pop_edges(i) + self.bias1[...]
        place = lax.broadcasted_iota(jnp.int32, (2 * EDGE, C), 0)
        outside = ((place % 2 == 0) & self.at_top) | ((place % 2 == 1) & self.at_bottom)
        hidden = jnp.where(outside, 0.0, hidden)
        values = normed(hidden, self.gain2[...]).astype(BF16).astype(F32)
        for j in range(2):
            f = 2 * i + j
            self.hidden_edges[f + 2] = jnp.where(f < self.live(), values[j * EDGE : (j + 1) * EDGE], 0.0)

    def final(self, f):
        result = self.pop_sums(1, f) + self.bias2[...] + self.x[f].astype(F32)
        return jnp.where(f < self.live(), result, 0.0).astype(BF16)

    def phase(self, conv, pair):
        if conv == 0:
            weights = [self.weights1.at[0], self.weights1.at[1], self.weights1_last]
        else:
            weights = [self.weights2.at[a] for a in range(3)]
        operand = (self.operand1, self.operand2)[conv]
        moved = conv in self.moved
        units = ([], [])

        def add(unit, taps, work, edge_work=()):
            work = [(accumulator, operand, g) for accumulator, g in work]
            if conv == 0:
                work += [(accumulator, self.edges, g) for accumulator, g in edge_work]
            units[unit].extend((unit, taps, step, weights, work) for step in range(STEPS))

        left, right = self.left[conv], self.right[conv]
        for a in range(3):
            work = [(left[g - a], g) for g in (pair, pair + 1) if 0 <= g - a < FRAMES]
            edge_work = [(self.left_edges[i], 2 * i + a) for i in range(2) if pair <= 2 * i + a + 1 < pair + 2]
            if work and not (moved and pair == 2 and a == 2):
                add(0, (a,), work, edge_work)
        edges = self.right_edges
        if pair == 0:
            add(1, (0, 1), [(right[0], 0), (right[1], 1)], [(edges[0], 0)])
        elif pair == 2:
            add(1, (0, 1), [(right[2], 2), (right[3], 3)], [(edges[2], 1), (edges[1], 2)])
            add(1, (None, 2), [(right[1], 2), (right[2], 3)], [(edges[2], 2)])
            if moved:
                add(1, (2,), [(self.moved_left[f], f + 2) for f in range(2)], [(self.moved_edges[0], 2)])
        else:
            add(1, (1, 2), [(right[3], 4), (right[4], 5)], [(edges[1], 3), (edges[3], 4)])
        return (conv, pair), units

    def run(self, order):
        steps = [[entry for entry in order if isinstance(entry, tuple) and entry[0] == unit] for unit in range(2)]
        count = [0, 0]

        def push(unit, i):
            _, taps, step, weights, _ = steps[unit][i]
            pltpu.matmul_push_rhs(weight_tile(weights, taps, step), i % 2, unit)

        for entry in order:
            if not isinstance(entry, tuple):
                entry()
                continue
            unit, _, step, _, work = entry
            i = count[unit]
            count[unit] += 1
            if i == 0:
                push(unit, 0)
            if i + 1 < len(steps[unit]):
                push(unit, i + 1)
            for n, (accumulator, operand, g) in enumerate(work):
                multiply(accumulator, operand, g, step, i % 2 if n == 0 else None)


def hand_out(upper, lower, even, near, far, f):
    near[f] = jnp.where(even, lower, upper).astype(BF16)
    far[f] = jnp.where(even, upper, lower).astype(BF16)


def edges_out(main, even, near, far, f):
    hand_out(rows_out(main, 0), rows_out(main, 6), even, near, far, f)


def pack_kernel(x, first, second, near, far):
    even = lax.axis_index("strip") % 2 == 0
    for source, start in ((first, 4), (x, 0)):
        for f in range(source.shape[0]):
            edges_out(source[f].astype(F32), even, near, far, start + f)
    frames = [second[f].astype(F32) for f in range(2)]
    upper, lower = ([rows_out(rows, at) for rows in frames] for at in (0, 6))
    upper = merged(upper[0], rolled(upper[1], 1, 0))
    lower = merged(rolled(lower[0], -1, 0), lower[1])
    hand_out(upper, lower, even, near, far, 6)


WINDOW = (FRAMES + 2, MAIN, C)
OPERANDS = dict(
    edge_rows=pltpu.VMEM((FRAMES + 2, 3, EDGE, C), F32),
    operand1=pltpu.VMEM((FRAMES + 2, MAIN, K), BF16),
    edges=pltpu.VMEM((FRAMES + 1, 2 * EDGE, K), BF16),
    operand2=pltpu.VMEM((FRAMES + 2, MAIN, K), BF16),
)
VECTORS = ("bias1", "gain1", "bias2", "gain2")


def live_frames(counts, tick):
    return counts[7 - lax.axis_index("segment") + tick]


ACCUMULATORS = dict(
    left=(0, MAIN, FRAMES + 2),
    left_edges=(0, 2 * EDGE, 2),
    right=(1, MAIN, FRAMES + 2),
    right_edges=(1, 2 * EDGE, 4),
    moved_left=(1, MAIN, 2),
    moved_edges=(1, 2 * EDGE, 1),
)


def with_section(given, body):
    strip = lax.axis_index("strip")
    given = {"early1": None, **given}

    def inner(*accumulators):
        body(Section(given, accumulators, strip % 2 == 0, strip == 0, strip == lax.axis_size("strip") - 1))

    shapes = [pltpu.ACC(unit)((rows, TILE), F32) for unit, rows, count in ACCUMULATORS.values() for _ in range(count)]
    pl.run_scoped(inner, *shapes)


def prepare_kernel(r):
    pairs = [(r[n + "_hbm"], r[n]) for n in ("x", "gain1", "bias1", "gain2", "bias2", "second", "incoming")]
    pairs += [(r["counts_hbm"], r["counts"]), (r["first_hbm"], r["window1"].at[pl.ds(0, 2)])]
    pairs += [(r["weights1_hbm"].at[a], r["weights1"].at[a]) for a in range(2)]
    copies = [pltpu.make_async_copy(source, target, r["sems"].at[i]) for i, (source, target) in enumerate(pairs)]
    for copy in copies:
        copy.start()
    copies[7].wait()
    copies[0].wait()
    copies[1].wait()
    live = live_frames(r["counts"], 0)
    gain = r["gain1"][...]
    for f in range(FRAMES):
        r["window1"][f + 2] = first_normed(r["x"][f], f < live, gain)
    for i, copy in enumerate(copies):
        if i not in (0, 1, 7):
            copy.wait()


def tick0_kernel(r):
    counting = pltpu.make_async_copy(r["counts_hbm"], r["counts"], r["sems"].at[3])
    counting.start()
    pairs = [(r["weights1_hbm"].at[2], r["weights1_last"])]
    pairs += [(r["weights2_hbm"].at[a], r["weights2"].at[a]) for a in range(3)]
    copies = [pltpu.make_async_copy(source, target, r["sems"].at[4 + i]) for i, (source, target) in enumerate(pairs)]
    for copy in copies:
        copy.start()

    def body(work):
        work.norms = False
        work.moved = (0, 1)
        work.live = lambda: live_frames(r["counts"], 0)
        work.window2[0:2] = work.second[...]
        for g in range(2):
            work.halos[g] = jnp.concatenate(work.halo(4 + g), axis=0).astype(BF16)
        top, bottom = work.halo(6)
        work.hidden_edges[0] = merged(top, rolled(bottom, 1, 0))
        work.hidden_edges[1] = merged(rolled(top, -1, 0), bottom)
        last = lax.axis_index("segment") == lax.axis_size("segment") - 1

        def finish(f):
            result = work.final(f)
            work.result[f] = result
            fresh = jnp.where(f < r["counts"][8], work.incoming[f].astype(F32), 0.0)
            passed = jnp.where(last, fresh, result.astype(F32))
            work.send[f] = passed.astype(BF16)
            edges_out(passed, work.even, work.send_near, work.send_far, f)

        finishing = [lambda f=f: finish(f) for f in range(FRAMES)]
        phases = [work.phase(conv, pair) for conv in range(2) for pair in (0, 2, 4)]
        groups = [
            (1280, (0, 2), [counting.wait] + work.first_thunks(2)),
            ((0, 0), (0, 4), work.first_thunks(4)),
            ((0, 0), (0, 4), work.second_thunks(0, cached=True)),
            ((0, 0), (0, 4), [copies[0].wait]),
            ((0, 2), (1, 0), [copy.wait for copy in copies[1:]]),
            ((0, 2), (1, 0), work.second_thunks(2)),
            ((0, 4), (1, 2), work.second_thunks(4)),
            ((1, 2), None, finishing[:2]),
        ]
        order = work.first_thunks(0, cached=True) + timeline(phases, groups)
        work.run(order + finishing[2:])

    with_section(r, body)


def between_kernel(r):
    writing = pltpu.make_async_copy(r["result"], r["whole"].at[0], r["sems"].at[0])
    writing.start()
    counting = pltpu.make_async_copy(r["counts_hbm"], r["counts"], r["sems"].at[1])
    counting.start()
    counting.wait()
    live = live_frames(r["counts"], 0)
    for i in range(2):
        r["first"][i] = r["window1_old"][live + i]
        r["first_halo"][i] = r["halos_old"][live + i]
        r["second"][i] = r["window2_old"][live + i]
        r["second_edge"][i] = r["edges_old"][live + i]

    def body(work):
        work.moved = ()

        def store(conv, sums):
            for f in range(2):
                right, second = halves(work.right[conv][f])
                if f == 1:
                    sums[0, :, TILE:C] += second
                sums[f, :, 0:TILE] = pltpu.matmul_pop(work.left[conv][f])
                sums[f, :, TILE:C] = right
            if conv == 0:
                work.sum_edges[:, 0:TILE] = pltpu.matmul_pop(work.left_edges[0])
                work.sum_edges[:, TILE:C] = halves(work.right_edges[0])[0]

        order = work.first_thunks(0, cached=True)
        order += timeline([work.phase(0, 0)], [(-1, None, work.second_thunks(0, cached=True))])
        order += [lambda: store(0, work.sum1)]
        order += timeline([work.phase(1, 0)], [])
        work.run(order)
        store(1, work.sum2)

    given = dict(r, window1=r["first"], halos=r["first_halo"], window2=r["second"], hidden_edges=r["second_edge"])
    with_section(given, body)
    writing.wait()


def tick1_kernel(r):
    counting = pltpu.make_async_copy(r["counts_hbm"], r["counts"], r["sems"].at[0])
    counting.start()
    copies = []

    def send(source, target):
        copies.append(pltpu.make_async_copy(source, target, r["sems"].at[len(copies) + 1]))
        copies[-1].start()

    def body(work):
        work.norms = True
        work.moved = (0,)
        work.live = lambda: live_frames(r["counts"], 1)
        for i in range(2):
            work.window1[i] = work.first[i]
            work.halos[i] = work.first_halo[i]
            work.window2[i] = work.second[i]
            work.hidden_edges[i] = work.second_edge[i]

        def finish(f):
            work.result[f] = work.final(f)
            send(work.result.at[f], work.whole.at[1, f])

        def send_window(window, target):
            send(window.at[pl.ds(work.live(), 2)], target)

        finishing = [lambda f=f: finish(f) for f in range(FRAMES)]
        phases = [work.phase(conv, pair) for conv in range(2) for pair in (2, 4)]
        groups = [
            (-1, (0, 4), work.first_thunks(4)),
            (-1, (0, 4), [counting.wait]),
            ((0, 2), (1, 2), work.second_thunks(2)),
            ((0, 2), (1, 2), [lambda: send_window(work.window1, work.first_next)]),
            ((0, 4), (1, 4), work.second_thunks(4)),
            ((1, 2), None, finishing[:2]),
        ]
        order = [lambda: work.build_first_edges(1)] + work.first_thunks(2) + timeline(phases, groups)
        work.run(order + [lambda: send_window(work.window2, work.second_next)] + finishing[2:])
        for copy in copies:
            copy.wait()

    with_section(r, body)


def call(kernel, operands, outputs, scratch, flops=0, moved=0):
    inputs = list(operands)
    names = inputs + list(outputs) + list(scratch)
    in_hbm = [n.endswith("_hbm") or n == "base" for n in inputs]
    values = [
        pltpu.with_memory_space_constraint(v, pltpu.HBM) if n.endswith("_hbm") else v for n, v in operands.items()
    ]
    aliases = {inputs.index("base"): list(outputs).index("whole")} if "base" in inputs else {}
    results = pl.pallas_call(
        lambda *refs: kernel(dict(zip(names, refs))),
        out_shape=list(outputs.values()),
        in_specs=[HBM if there else VMEM for there in in_hbm],
        out_specs=[HBM if n in ("whole", "first_next", "second_next") else VMEM for n in outputs],
        input_output_aliases=aliases,
        scratch_shapes=list(scratch.values()),
        compiler_params=pltpu.CompilerParams(vmem_limit_bytes=22 << 20),
        cost_estimate=pl.CostEstimate(flops=flops, bytes_accessed=moved, transcendentals=0),
        name=kernel.__name__.removesuffix("_kernel"),
    )(*values)
    return dict(zip(outputs, results))


def shape(*dims):
    return jax.ShapeDtypeStruct(dims, BF16)


def flat(array):
    frames = array.shape[0]
    return array.transpose(0, 2, 1, 3).reshape(frames, MAIN, C)


def unflat(array):
    frames = array.shape[0]
    return array.reshape(frames, COLS, ROWS, C).transpose(0, 2, 1, 3)


def on_device(
    held_blocks,
    incoming,
    frame_counts,
    first_cache,
    second_cache,
    first_kernel,
    first_bias,
    first_gain,
    second_kernel,
    second_bias,
    second_gain,
):
    segments = lax.axis_size("segment")
    strips = lax.axis_size("strip")
    axes = ("segment", "strip")

    def swap(rows, far, step):
        pairs = []
        for s in range(segments):
            for k in range(strips):
                to, into = (((k + 1) ^ 1) - 1 if far else k ^ 1), (s + step) % segments
                if not 0 <= to < strips:
                    to, into = k, (into if step else s ^ 1)
                pairs.append((s * strips + k, into * strips + to))
        return lax.ppermute(rows, axes, pairs)

    x = flat(held_blocks[0])
    first = flat(first_cache[0])
    second = flat(second_cache[0])
    near, far = pl.pallas_call(
        pack_kernel,
        out_shape=[pltpu.VMEM((7, EDGE, C), BF16)] * 2,
        in_specs=[VMEM] * 3,
        out_specs=[VMEM] * 2,
        compiler_params=pltpu.CompilerParams(vmem_limit_bytes=8 << 20),
        name="pack",
    )(*(pltpu.with_memory_space_constraint(rows, pltpu.HBM) for rows in (x, first, second)))
    far = swap(far, True, 0)
    near = swap(near, False, 0)
    counts = dict(counts_hbm=frame_counts)
    count_scratch = dict(counts=pltpu.SMEM((9,), jnp.int32), sems=pltpu.SemaphoreType.DMA((16,)))
    block = pltpu.VMEM((FRAMES, MAIN, C), BF16)
    cached = pltpu.VMEM((2, MAIN, C), BF16)
    weights = pltpu.VMEM((3, K, C), BF16)
    ready = call(
        prepare_kernel,
        dict(
            x_hbm=x,
            first_hbm=first,
            second_hbm=second,
            incoming_hbm=flat(incoming[0]),
            bias1_hbm=first_bias,
            gain1_hbm=first_gain,
            bias2_hbm=second_bias,
            gain2_hbm=second_gain,
            weights1_hbm=first_kernel[0].reshape(3, K, C),
            **counts,
        ),
        dict(
            x=block,
            second=cached,
            incoming=block,
            window1=pltpu.VMEM(WINDOW, BF16),
            weights1=pltpu.VMEM((2, K, C), BF16),
            **{n: pltpu.VMEM((1, C), F32) for n in VECTORS},
        ),
        count_scratch,
        moved=2 * 2 * K * C,
    )
    vectors = {n: ready[n] for n in VECTORS}
    done = call(
        tick0_kernel,
        dict(
            **counts,
            far=far,
            near=near,
            weights1_hbm=first_kernel[0].reshape(3, K, C),
            weights2_hbm=second_kernel[0].reshape(3, K, C),
            **ready,
        ),
        dict(
            weights1_last=pltpu.VMEM((K, C), BF16),
            weights2=weights,
            halos=pltpu.VMEM((FRAMES + 2, 2 * EDGE, C), BF16),
            window2=pltpu.VMEM(WINDOW, BF16),
            hidden_edges=pltpu.VMEM((FRAMES + 2, EDGE, C), F32),
            result=block,
            send=shape(FRAMES, MAIN, C),
            send_near=shape(FRAMES, EDGE, C),
            send_far=shape(FRAMES, EDGE, C),
        ),
        {**OPERANDS, **count_scratch},
    )

    onward = [(s * strips + k, (s + 1) % segments * strips + k) for s in range(segments) for k in range(strips)]
    far = swap(done["send_far"], True, 1)
    near = swap(done["send_near"], False, 1)
    x = lax.ppermute(done["send"], axes, onward)
    both = dict(weights1=ready["weights1"], **{n: done[n] for n in ("weights1_last", "weights2")})
    early = call(
        between_kernel,
        dict(
            **counts,
            window1_old=ready["window1"],
            halos_old=done["halos"],
            window2_old=done["window2"],
            edges_old=done["hidden_edges"],
            result=done["result"],
            **both,
        ),
        dict(
            whole=shape(2, FRAMES, MAIN, C),
            first=cached,
            first_halo=pltpu.VMEM((2, 2 * EDGE, C), BF16),
            second=cached,
            second_edge=pltpu.VMEM((2, EDGE, C), F32),
            sum1=pltpu.VMEM((2, MAIN, C), F32),
            sum_edges=pltpu.VMEM((2 * EDGE, C), F32),
            sum2=pltpu.VMEM((2, MAIN, C), F32),
        ),
        {**OPERANDS, **count_scratch},
        flops=2 * 2 * 3 * MAIN * K * C,
        moved=2 * 3 * K * C,
    )
    whole = early.pop("whole")
    for name, sums in (("early1", "sum1"), ("early_edges", "sum_edges"), ("early2", "sum2")):
        early[name] = early.pop(sums)
    out = call(
        tick1_kernel,
        dict(**counts, far=far, near=near, x=x, **early, **both, **vectors, base=whole),
        dict(whole=shape(2, FRAMES, MAIN, C), first_next=shape(2, MAIN, C), second_next=shape(2, MAIN, C)),
        dict(
            window1=pltpu.VMEM(WINDOW, BF16),
            halos=pltpu.VMEM((FRAMES + 2, 2 * EDGE, C), BF16),
            window2=pltpu.VMEM(WINDOW, BF16),
            hidden_edges=pltpu.VMEM((FRAMES + 2, EDGE, C), F32),
            result=block,
            **OPERANDS,
            **count_scratch,
        ),
    )
    return (
        unflat(out["whole"].reshape(2 * FRAMES, MAIN, C)).reshape(2, 1, FRAMES, ROWS, COLS, C),
        unflat(out["first_next"])[None],
        unflat(out["second_next"])[None],
    )


def solution(mesh):
    return jax.shard_map(
        on_device,
        mesh=mesh,
        in_specs=(
            P("segment", None, "strip", None, None),
            P(None, None, "strip", None, None),
            P(),
            P("segment", None, "strip", None, None),
            P("segment", None, "strip", None, None),
            P("segment", None, None, None, None, None),
            P("segment", None),
            P("segment", None),
            P("segment", None, None, None, None, None),
            P("segment", None),
            P("segment", None),
        ),
        out_specs=(
            P(None, "segment", None, "strip", None, None),
            P("segment", None, "strip", None, None),
            P("segment", None, "strip", None, None),
        ),
        check_vma=False,
    )
```
